32 devices in a mesh: zrow: 4 (over z), zcol: 8 (over y, x, core).
Axes of the slice: x: 2, y: 2, z: 4, core: 2. Of those that a mesh axis runs over, the one named last changes fastest.
Arguments:
- state: float32 [64, 8, 32768], P(None, None, ('zrow', 'zcol')), may hold values from -6 to 6
- kernel: float32 [32768], P(('zrow', 'zcol')), may hold values from 0.5 to 5
- blocks: int32 [2048, 4], replicated, may hold values from 0 to 255
- foot_weight: float32 [2048, 4], replicated, may hold values from 0.2 to 1
- bin_response: float32 [2048, 8], replicated, may hold values from 0.1 to 1
- observed: float32 [2048, 64], replicated, may hold values from -6 to 6
- obs_var: float32 [2048], replicated, may hold values from 0.1 to 1
- batch_order: int32 [2048], replicated, may hold values from 0 to 2047, each once
Outputs:
- analysis: float32 [64, 8, 32768], P(None, None, ('zrow', 'zcol'))
- obs_analysis: float32 [2, 64, 1024], P(None, None, ('zrow', 'zcol'))
The draws below stay inside these ranges and needn't reach their ends.
All inputs are finite; a program needn't handle non-finite values.
Results may differ from the reference program's by a relative error of at most 0.0003.
Values sent between devices are 32-bit elements; how exact they have to be, the bound alone decides.
No kernel may reach another device: no remote copies, remote signals or barrier semaphores. Data moves between devices by JAX's collectives and lax.ppermute only.
A program may use at most 128 MiB of HBM per device.

```python
import math
import jax
import jax.numpy as jnp
from jax import lax

M = 64
BINS = 8
BLK = 128
FOOT = 4
P_SIZE = 1024
BATCHES = 2
NCELLS = 32768
NBLK = 256
SENSORS = 2048


def with_ends(drawn, own_key, low, largest):
    index_at = [jax.random.randint(jax.random.fold_in(own_key, axis), (), 0, length) for axis, length in enumerate(drawn.shape)]
    widest = drawn.shape.index(max(drawn.shape))
    next_to = index_at[:widest] + [(index_at[widest] + 1) % drawn.shape[widest]] + index_at[widest + 1:]
    return drawn.at[tuple(index_at)].set(low).at[tuple(next_to)].set(largest)


def shard_levels(stream_key, dims, shards, least, top_value):
    level, own = 1.0, jax.random.fold_in(stream_key, 6)
    for axis_at, blocks in shards:
        heights = jnp.exp(jax.random.uniform(jax.random.fold_in(own, axis_at), (blocks,), jnp.float32, least / len(shards), top_value / len(shards)))
        level = level * jnp.repeat(heights, dims[axis_at] // blocks).reshape([-1 if axis == axis_at else 1 for axis in range(len(dims))])
    return level


def bell_draw(own_key, extent, deviation, limit, split=(), kind=jnp.bfloat16):
    array = jax.random.normal(own_key, extent, jnp.float32) * deviation
    if len(split) > 0:
        array = shard_levels(own_key, extent, split, -0.22, 0.18) * array
    return jnp.clip(array, min=-limit, max=limit).astype(kind)


def setup_inputs(seed: int = 0) -> dict:
    keys = jax.random.split(jax.random.key(seed), 9)
    state = bell_draw(keys[0], (M, BINS, NCELLS), 1.0, 6.0, ((2, 32),), jnp.float32)
    kernel = jnp.clip(jnp.exp(math.log(5.0) - 2.3025851 * jax.random.uniform(keys[1], (NCELLS,), jnp.float32) ** shard_levels(keys[1], (NCELLS,), ((0, 32),), -0.2, 0.2)), 0.5, 5.0)
    blocks = with_ends(jax.random.randint(keys[2], (SENSORS, FOOT), 0, NBLK), jax.random.fold_in(keys[2], 1), 0, NBLK - 1).astype(jnp.int32)
    foot_weight = jnp.clip(jax.random.uniform(keys[3], (SENSORS, FOOT), jnp.float32, 0.2, 1.0), 0.2, 1.0)
    bin_response = jnp.clip(jnp.exp(jax.random.uniform(keys[4], (SENSORS, BINS), jnp.float32, math.log(0.1), math.log(1.0))), 0.1, 1.0)
    observed = bell_draw(keys[5], (SENSORS, M), 1.0, 6.0, (), jnp.float32)
    obs_var = jnp.clip(jnp.exp(jax.random.uniform(keys[6], (SENSORS,), jnp.float32, math.log(0.1), math.log(1.0))), 0.1, 1.0)
    batch_order = jax.random.permutation(keys[7], SENSORS).astype(jnp.int32)
    return dict(state=state, kernel=kernel, blocks=blocks, foot_weight=foot_weight, bin_response=bin_response, observed=observed, obs_var=obs_var, batch_order=batch_order)


def block_means(field, kernel):
    weighted = field.reshape(M, BINS, NBLK, BLK) * kernel.reshape(NBLK, BLK)
    return jnp.sum(weighted, axis=3) / BLK

def observe(means, sensor_blocks, sensor_foot, sensor_bins):
    picked = means[:, :, sensor_blocks]
    return jnp.einsum('mbpf,pf,pb->mp', picked, sensor_foot, sensor_bins, precision=lax.Precision.HIGHEST)

def gain_of(hx, sensor_obs, sensor_var):
    anom = hx - jnp.mean(hx, axis=0, keepdims=True)
    depart = sensor_obs.T - hx
    cov = jnp.dot(anom.T, anom, precision=lax.Precision.HIGHEST) / (M - 1) + jnp.diag(sensor_var)
    factor = jnp.linalg.cholesky(cov)
    solved = jax.scipy.linalg.cho_solve((factor, True), depart.T)
    return jnp.dot(anom, solved, precision=lax.Precision.HIGHEST) / (M - 1)

def reference(state, kernel, blocks, foot_weight, bin_response, observed, obs_var, batch_order):
    field = state
    center = jnp.eye(M, dtype=jnp.float32) - 1.0 / M
    for batch in range(BATCHES):
        chosen = batch_order[batch * P_SIZE:(batch + 1) * P_SIZE]
        hx = observe(block_means(field, kernel), blocks[chosen], foot_weight[chosen], bin_response[chosen])
        gain = gain_of(hx, observed[chosen], obs_var[chosen])
        mixer = jnp.eye(M, dtype=jnp.float32) + jnp.dot(gain.T, center, precision=lax.Precision.HIGHEST)
        field = jnp.dot(mixer, field.reshape(M, -1), precision=lax.Precision.HIGHEST).reshape(M, BINS, NCELLS)
    means = block_means(field, kernel)
    finals = []
    for batch in range(BATCHES):
        chosen = batch_order[batch * P_SIZE:(batch + 1) * P_SIZE]
        finals.append(observe(means, blocks[chosen], foot_weight[chosen], bin_response[chosen]))
    return (field, jnp.stack(finals))
```

```python
import functools

import jax
import jax.numpy as jnp
from jax import lax
from jax.experimental import pallas as pl
from jax.experimental.pallas import tpu as pltpu
from jax.sharding import PartitionSpec as P

BLK = 128
P_SIZE = 1024
AXES = ("zrow", "zcol")
F32 = jnp.float32
BF16 = jnp.bfloat16
NT = (((1,), (1,)), ((), ()))
VMEM_SPEC = pl.BlockSpec(memory_space=pltpu.VMEM)
LIMIT = 56 * 1024 * 1024


def split(x):
    hi = x.astype(BF16)
    return hi, (x - hi.astype(F32)).astype(BF16)


def mm(a, b):
    return jnp.dot(a, b, precision=lax.Precision.HIGHEST, preferred_element_type=F32)


def means_kernel(x_ref, kernel_ref, out_ref):
    nb, cells = out_ref.shape[0], x_ref.shape[1]
    row = lax.broadcasted_iota(jnp.int32, (nb, cells), 0)
    col = lax.broadcasted_iota(jnp.int32, (nb, cells), 1)
    lo = row * BLK
    picked = jnp.where((col >= lo) & (col < lo + BLK), kernel_ref[...] * (1.0 / BLK), 0.0)
    out_ref[...] = lax.dot_general(
        picked, x_ref[...], NT, precision=lax.Precision.HIGHEST, preferred_element_type=F32
    )


def spread_kernel(bits, nb, me_ref, blocks_ref, weight_ref, out_ref):
    foot, sensors = blocks_ref.shape
    slots = out_ref.shape[1]
    step = 128
    for c in range(0, sensors, step):
        blk = blocks_ref[:, c : c + step]
        away = lax.shift_right_logical(blk, nb.bit_length() - 1) ^ me_ref[0]
        place = blk & (nb - 1)
        for i, bit in enumerate(bits):
            place += (lax.shift_right_logical(away, bit) & 1) * (nb << i)
        weight = weight_ref[:, c : c + step]
        for r in range(0, slots, 256):
            row = lax.broadcasted_iota(jnp.int32, (256, step), 0) + r
            total = jnp.zeros((256, step), F32)
            for f in range(foot):
                total += jnp.where(row == place[f : f + 1, :], weight[f : f + 1, :], 0.0)
            hi, low = split(total)
            out_ref[0, r : r + 256, c : c + step] = hi
            out_ref[1, r : r + 256, c : c + step] = low


def halves_kernel(members, bins, x_ref, hi_ref, lo_ref):
    for b in range(bins):
        hi, low = split(x_ref[:, b, :])
        hi_ref[b] = hi
        lo_ref[b] = low


def sublane_mean(x):
    return jnp.sum(x, axis=0, keepdims=True) * (1.0 / x.shape[0])


def lane_mean(x):
    return jnp.sum(x, axis=1, keepdims=True) * (1.0 / x.shape[1])


def solve(aug):
    n = aug.shape[0]
    width = aug.shape[1]
    rows = [aug[8 * i : 8 * i + 8, :] for i in range(n // 8)]
    sub = lax.broadcasted_iota(jnp.int32, (8, width), 0)

    def lanes(x, j):
        return jnp.broadcast_to(x[:, j : j + 1], (8, width))

    for k in range(n // 8):
        piv = rows[k]
        own = [lanes(piv, 8 * k + q) for q in range(8)]
        for q in range(8):
            here = sub == q
            mult = own[q]
            inv = 1.0 / mult[q : q + 1, :]
            scaled = piv[q : q + 1, :] * inv
            piv = jnp.where(here, scaled, piv - mult * scaled)
            for p in range(q + 1, 8):
                scaled = own[p][q : q + 1, :] * inv
                own[p] = jnp.where(here, scaled, own[p] - mult * scaled)
        for i in range(n // 8):
            if i != k:
                new = rows[i]
                for q in range(8):
                    new = new - lanes(rows[i], 8 * k + q) * piv[q : q + 1, :]
                rows[i] = new
        rows[k] = piv
    return jnp.concatenate(rows, axis=0)[:, n:]


def update_kernel(
    members, bins, gathered_ref, spread_ref, resp_ref, obs_ref, weight_ref, own_ref, xhi_ref, xlo_ref,
    field_ref, finals_ref, turned, left, anom, depart,
):
    slots = gathered_ref.shape[0]
    sensors = resp_ref.shape[1]
    rows = members * bins
    for r in range(0, slots, 128):
        turned[...] = gathered_ref[r : r + 128, :].T
        for b in range(bins):
            hi, low = split(turned[pl.ds(b, members, stride=bins), :])
            left[0, b * members : (b + 1) * members, r : r + 128] = hi
            left[1, b * members : (b + 1) * members, r : r + 128] = low
    step = 256
    for c in range(0, sensors, step):
        z = (
            jnp.dot(left[0], spread_ref[0, :, c : c + step], preferred_element_type=F32)
            + jnp.dot(left[0], spread_ref[1, :, c : c + step], preferred_element_type=F32)
            + jnp.dot(left[1], spread_ref[0, :, c : c + step], preferred_element_type=F32)
        )
        hx = z[0:members, :] * resp_ref[0:1, c : c + step]
        for b in range(1, bins):
            hx += z[b * members : (b + 1) * members, :] * resp_ref[b : b + 1, c : c + step]
        center = sublane_mean(hx)
        anom[0:members, c : c + step] = hx - center
        anom[members : 2 * members, c : c + step] = obs_ref[:, c : c + step] - center
        depart[:, c : c + step] = hx
    ahi, alo = split(anom[...])
    wide = jnp.concatenate(
        [anom[0:members, :] * weight_ref[t : t + 1, :] for t in range(2)], axis=0
    )
    whi, wlo = split(wide)
    sums = (
        lax.dot_general(whi, ahi, NT, preferred_element_type=F32)
        + lax.dot_general(whi, alo, NT, preferred_element_type=F32)
        + lax.dot_general(wlo, ahi, NT, preferred_element_type=F32)
    )
    r64 = lax.broadcasted_iota(jnp.int32, (members, members), 0)
    c64 = lax.broadcasted_iota(jnp.int32, (members, members), 1)
    eye = (r64 == c64).astype(F32)
    s0, e0 = sums[0:members, 0:members], sums[0:members, members:]
    s1, e1 = sums[members:, 0:members], sums[members:, members:]
    gain = solve(jnp.concatenate([s0 + (members - 1.0) * eye, e0 - s0], axis=1))
    first_t = eye + gain - sublane_mean(gain)
    first_ct = first_t - lane_mean(first_t)
    first = first_t.T
    first_c = first - sublane_mean(first)
    prod = mm(s1, jnp.concatenate([first_ct, first_t], axis=1))
    aug = mm(first_c, jnp.concatenate([prod[:, 0:members], e1 - prod[:, members:]], axis=1))
    gain = solve(
        jnp.concatenate([aug[:, 0:members] + (members - 1.0) * eye, aug[:, members:]], axis=1)
    )
    total = first + mm(gain.T, first_c)
    thi, tlo = split(total)
    for b in range(bins):
        out = (
            jnp.dot(thi, xhi_ref[b], preferred_element_type=F32)
            + jnp.dot(thi, xlo_ref[b], preferred_element_type=F32)
            + jnp.dot(tlo, xhi_ref[b], preferred_element_type=F32)
        )
        field_ref[:, b, :] = out
    nown = own_ref.shape[0]
    sensor = lax.broadcasted_iota(jnp.int32, (nown, sensors), 1)
    onehot = (sensor == own_ref[...]).astype(BF16)
    hhi, hlo = split(depart[...])
    hlo2 = (depart[...] - hhi.astype(F32) - hlo.astype(F32)).astype(BF16)
    picked = (
        lax.dot_general(onehot, hhi, NT, preferred_element_type=F32)
        + lax.dot_general(onehot, hlo, NT, preferred_element_type=F32)
        + lax.dot_general(onehot, hlo2, NT, preferred_element_type=F32)
    )
    finals_ref[...] = lax.dot_general(
        picked, total, NT, precision=lax.Precision.HIGHEST, preferred_element_type=F32
    )


def shards(state, kernel, blocks, foot_weight, bin_response, observed, obs_var, batch_order):
    members, bins, cells = state.shape
    nb = cells // BLK
    sensors = obs_var.shape[0]
    batches = sensors // P_SIZE
    nz, nc = lax.axis_size("zrow"), lax.axis_size("zcol")
    devices = nz * nc
    me = lax.axis_index(AXES)
    share = P_SIZE // devices
    zbits = [(nc << i).bit_length() - 1 for i in range(nz.bit_length() - 1)]
    cbits = [i for i in reversed(range(nc.bit_length() - 1))]
    bits = zbits + cbits
    rows = members * bins
    params = pltpu.CompilerParams(vmem_limit_bytes=LIMIT)

    flat = state.reshape(rows, cells)
    piece = pl.pallas_call(
        means_kernel,
        out_shape=jax.ShapeDtypeStruct((nb, rows), F32),
        in_specs=[VMEM_SPEC, VMEM_SPEC],
        out_specs=VMEM_SPEC,
        compiler_params=params,
        name="means",
    )(flat, kernel.reshape(1, cells))
    for bit in bits:
        other = lax.ppermute(piece, AXES, [(i, i ^ (1 << bit)) for i in range(devices)])
        piece = jnp.concatenate([piece, other], axis=0)

    slots = nb * devices
    spread = pl.pallas_call(
        functools.partial(spread_kernel, bits, nb),
        out_shape=jax.ShapeDtypeStruct((2, slots, sensors), BF16),
        in_specs=[pl.BlockSpec(memory_space=pltpu.SMEM), VMEM_SPEC, VMEM_SPEC],
        out_specs=VMEM_SPEC,
        compiler_params=params,
        name="spread",
        cost_estimate=pl.CostEstimate(flops=2000000, bytes_accessed=3000000, transcendentals=0),
    )(me.reshape(1), blocks.T, foot_weight.T)
    xhi, xlo = pl.pallas_call(
        functools.partial(halves_kernel, members, bins),
        out_shape=[jax.ShapeDtypeStruct((bins, members, cells), BF16)] * 2,
        in_specs=[VMEM_SPEC],
        out_specs=[VMEM_SPEC, VMEM_SPEC],
        compiler_params=params,
        name="halves",
        cost_estimate=pl.CostEstimate(flops=2000000, bytes_accessed=4000000, transcendentals=0),
    )(state)
    orders = batch_order.reshape(batches, P_SIZE)
    member_of = jnp.any(
        orders[:, :, None] == jnp.arange(sensors, dtype=jnp.int32)[None, None, :], axis=1
    )
    weight = jnp.where(member_of, 1.0 / obs_var[None, :], 0.0)
    own = lax.dynamic_slice_in_dim(orders, me * share, share, 1).reshape(batches * share, 1)

    field, finals = pl.pallas_call(
        functools.partial(update_kernel, members, bins),
        out_shape=[
            jax.ShapeDtypeStruct((members, bins, cells), F32),
            jax.ShapeDtypeStruct((batches * share, members), F32),
        ],
        in_specs=[VMEM_SPEC] * 8,
        out_specs=[VMEM_SPEC, VMEM_SPEC],
        scratch_shapes=[
            pltpu.VMEM((rows, 128), F32),
            pltpu.VMEM((2, rows, slots), BF16),
            pltpu.VMEM((2 * members, sensors), F32),
            pltpu.VMEM((members, sensors), F32),
        ],
        compiler_params=params,
        name="update",
    )(piece, spread, bin_response.T, observed.T, weight, own, xhi, xlo)
    return (
        field,
        finals.reshape(batches, share, members).transpose(0, 2, 1),
    )


def solution(mesh):
    return jax.shard_map(
        shards,
        mesh=mesh,
        in_specs=(
            P(None, None, AXES),
            P(AXES),
            P(),
            P(),
            P(),
            P(),
            P(),
            P(),
        ),
        out_specs=(P(None, None, AXES), P(None, None, AXES)),
        check_vma=False,
    )
```

```python
import functools

import jax
import jax.numpy as jnp
from jax import lax
from jax.experimental import pallas as pl
from jax.experimental.pallas import tpu as pltpu
from jax.sharding import PartitionSpec as P

BLK = 128
P_SIZE = 1024
AXES = ("zrow", "zcol")
F32 = jnp.float32
BF16 = jnp.bfloat16
NT = (((1,), (1,)), ((), ()))
VMEM_SPEC = pl.BlockSpec(memory_space=pltpu.VMEM)
HBM_SPEC = pl.BlockSpec(memory_space=pltpu.HBM)
SMEM_SPEC = pl.BlockSpec(memory_space=pltpu.SMEM)
MIB = 1024 * 1024


def split(x):
    hi = x.astype(BF16)
    return hi, (x - hi.astype(F32)).astype(BF16)


def mm(a, b):
    return jnp.dot(a, b, precision=lax.Precision.HIGHEST, preferred_element_type=F32)


def sublane_mean(x):
    return jnp.sum(x, axis=0, keepdims=True) * (1.0 / x.shape[0])


def lane_mean(x):
    return jnp.sum(x, axis=1, keepdims=True) * (1.0 / x.shape[1])


def means_kernel(x_ref, kernel_ref, out_ref, held_ref, sems):
    members, bins, _ = x_ref.shape
    nb = out_ref.shape[0]
    copies = []
    for b in range(bins):
        copies.append(pltpu.make_async_copy(x_ref.at[:, b, :], held_ref.at[b], sems.at[b]))
        copies[-1].start()
    scale = kernel_ref[...] * (1.0 / BLK)
    lane = lax.broadcasted_iota(jnp.int32, (2 * members, 128), 1)
    for b in range(0, bins, 2):
        copies[b].wait()
        copies[b + 1].wait()
        total = jnp.zeros((2 * members, 128), F32)
        for j in range(nb):
            cut = slice(j * BLK, (j + 1) * BLK)
            x = jnp.concatenate([held_ref[b, :, cut], held_ref[b + 1, :, cut]], axis=0)
            summed = jnp.sum(x * scale[:, cut], axis=1, keepdims=True)
            total = jnp.where(lane == j, summed, total)
        out_ref[:, b * members : (b + 2) * members] = total.T[0:nb, :]


def spread_kernel(bits, nb, first, me_ref, blocks_ref, weight_ref, out_ref):
    foot, sensors = blocks_ref.shape
    half = out_ref.shape[0] // 3
    step = 128
    for c in range(0, sensors, step):
        blk = blocks_ref[:, c : c + step]
        away = lax.shift_right_logical(blk, nb.bit_length() - 1) ^ me_ref[0]
        place = blk & (nb - 1)
        for i, bit in enumerate(bits):
            place += (lax.shift_right_logical(away, bit) & 1) * (nb << i)
        weight = weight_ref[:, c : c + step]
        for r in range(0, half, 128):
            row = lax.broadcasted_iota(jnp.int32, (128, step), 0) + (r + first)
            total = jnp.where(row == place[0:1, :], weight[0:1, :], 0.0)
            for f in range(1, foot):
                total += jnp.where(row == place[f : f + 1, :], weight[f : f + 1, :], 0.0)
            hi, low = split(total)
            out_ref[r : r + 128, c : c + step] = hi
            out_ref[half + r : half + r + 128, c : c + step] = low
            out_ref[2 * half + r : 2 * half + r + 128, c : c + step] = hi


def halves_kernel(x_ref, out_ref, held_ref, sems):
    members, bins, _ = x_ref.shape
    copies = []
    for b in range(bins):
        copies.append(pltpu.make_async_copy(x_ref.at[:, b, :], held_ref.at[b], sems.at[b]))
        copies[-1].start()
    for b in range(bins):
        copies[b].wait()
        hi, low = split(held_ref[b])
        out_ref[b, 0:members, :] = hi
        out_ref[b, members : 2 * members, :] = low
        out_ref[b, 2 * members : 3 * members, :] = hi


def roles_kernel(orders_ref, own_ref, var_ref, weight_ref, pick_ref):
    batches, per = orders_ref.shape
    groups = var_ref.shape[0]
    inverse = 1.0 / var_ref[...]
    high = lax.broadcasted_iota(jnp.int32, (groups, per), 0)
    low = lax.broadcasted_iota(jnp.int32, (128, per), 0)
    for t in range(batches):
        order = orders_ref[t : t + 1, :]
        of_high = jnp.where(high == lax.shift_right_logical(order, 7), 1.0, 0.0).astype(BF16)
        of_low = jnp.where(low == (order & 127), 1.0, 0.0).astype(BF16)
        held = lax.dot_general(of_high, of_low, NT, preferred_element_type=F32) * inverse
        for g in range(groups):
            weight_ref[t : t + 1, g * 128 : (g + 1) * 128] = held[g : g + 1, :]
    sensors, nown = pick_ref.shape
    sensor = lax.broadcasted_iota(jnp.int32, (sensors, nown), 0)
    pick_ref[...] = jnp.where(sensor == own_ref[...], 1.0, 0.0).astype(BF16)


def turn(gathered_ref, left):
    half = gathered_ref.shape[0]
    for r in range(0, half, 128):
        hi, low = split(gathered_ref[r : r + 128, :].T)
        left[:, r : r + 128] = hi
        left[:, half + r : half + r + 128] = hi
        left[:, 2 * half + r : 2 * half + r + 128] = low


def observe(members, bins, left, spread_ref, resp_ref, cut):
    z = jnp.dot(left[...], spread_ref[:, cut], preferred_element_type=F32)
    hx = z[0:members, :] * resp_ref[0:1, cut]
    for b in range(1, bins):
        hx += z[b * members : (b + 1) * members, :] * resp_ref[b : b + 1, cut]
    return hx


def partial_kernel(members, bins, gathered_ref, spread_ref, resp_ref, hx_ref, left):
    turn(gathered_ref, left)
    step = 256
    for c in range(0, resp_ref.shape[1], step):
        cut = slice(c, c + step)
        hx_ref[:, cut] = observe(members, bins, left, spread_ref, resp_ref, cut)


def solve(aug):
    n = aug.shape[0]
    width = aug.shape[1]
    rows = [aug[8 * i : 8 * i + 8, :] for i in range(n // 8)]
    sub = lax.broadcasted_iota(jnp.int32, (8, width), 0)

    def lanes(x, j):
        return jnp.broadcast_to(x[:, j : j + 1], (8, width))

    for k in range(n // 8):
        piv = rows[k]
        own = [lanes(piv, 8 * k + q) for q in range(8)]
        for q in range(8):
            here = sub == q
            mult = own[q]
            inv = 1.0 / mult[q : q + 1, :]
            scaled = piv[q : q + 1, :] * inv
            piv = jnp.where(here, scaled, piv - mult * scaled)
            for p in range(q + 1, 8):
                scaled = own[p][q : q + 1, :] * inv
                own[p] = jnp.where(here, scaled, own[p] - mult * scaled)
        for i in range(n // 8):
            if i != k:
                new = rows[i]
                for q in range(8):
                    new = new - lanes(rows[i], 8 * k + q) * piv[q : q + 1, :]
                rows[i] = new
        rows[k] = piv
    return jnp.concatenate(rows, axis=0)[:, n:]


def update_kernel(
    members, bins, hx_ref, gathered_ref, spread_ref, resp_ref, obs_ref, weight_ref, pick_ref, x_ref,
    field_ref, finals_ref, left, out, sems,
):
    sensors = resp_ref.shape[1]
    turn(gathered_ref, left)
    step = 256
    sums = jnp.zeros((2 * members, 2 * members), F32)
    picked = jnp.zeros((2 * members, pick_ref.shape[1]), F32)
    for c in range(0, sensors, step):
        cut = slice(c, c + step)
        hx = hx_ref[:, cut] + observe(members, bins, left, spread_ref, resp_ref, cut)
        center = sublane_mean(hx)
        anom = hx - center
        right = jnp.concatenate([anom, obs_ref[:, cut] - center], axis=0)
        wide = jnp.concatenate([anom * weight_ref[t : t + 1, cut] for t in range(2)], axis=0)
        rhi, rlo = split(right)
        whi, wlo = split(wide)
        sums += lax.dot_general(
            jnp.concatenate([whi, whi, wlo], axis=1),
            jnp.concatenate([rhi, rlo, rhi], axis=1),
            NT,
            preferred_element_type=F32,
        )
        hhi, hlo = split(hx)
        picked += jnp.dot(
            jnp.concatenate([hhi, hlo], axis=0), pick_ref[cut, :], preferred_element_type=F32
        )
    picked = picked[0:members] + picked[members:]
    r64 = lax.broadcasted_iota(jnp.int32, (members, members), 0)
    c64 = lax.broadcasted_iota(jnp.int32, (members, members), 1)
    eye = (r64 == c64).astype(F32)
    s0, e0 = sums[0:members, 0:members], sums[0:members, members:]
    s1, e1 = sums[members:, 0:members], sums[members:, members:]
    gain = solve(jnp.concatenate([s0 + (members - 1.0) * eye, e0 - s0], axis=1))
    first_t = eye + gain - sublane_mean(gain)
    first_ct = first_t - lane_mean(first_t)
    first = first_t.T
    first_c = first - sublane_mean(first)
    prod = mm(s1, jnp.concatenate([first_ct, first_t], axis=1))
    aug = mm(first_c, jnp.concatenate([prod[:, 0:members], e1 - prod[:, members:]], axis=1))
    gain = solve(
        jnp.concatenate([aug[:, 0:members] + (members - 1.0) * eye, aug[:, members:]], axis=1)
    )
    total = first + mm(gain.T, first_c)
    thi, tlo = split(total)
    both = jnp.concatenate([thi, thi, tlo], axis=1)
    copies = []
    for b in range(bins):
        out[b] = jnp.dot(both, x_ref[b], preferred_element_type=F32)
        copies.append(pltpu.make_async_copy(out.at[b], field_ref.at[:, b, :], sems.at[b]))
        copies[-1].start()
    finals_ref[...] = mm(total, picked).T
    for copy in copies:
        copy.wait()


def shards(state, kernel, blocks, foot_weight, bin_response, observed, obs_var, batch_order):
    members, bins, cells = state.shape
    nb = cells // BLK
    sensors = obs_var.shape[0]
    batches = sensors // P_SIZE
    nz, nc = lax.axis_size("zrow"), lax.axis_size("zcol")
    devices = nz * nc
    me = lax.axis_index(AXES)
    share = P_SIZE // devices
    zbits = [(nc << i).bit_length() - 1 for i in range(nz.bit_length() - 1)]
    cbits = [i for i in reversed(range(nc.bit_length() - 1))]
    bits = zbits + cbits
    rows = members * bins
    half = nb * devices // 2
    wide = 6 * half * sensors
    small = pltpu.CompilerParams(vmem_limit_bytes=8 * MIB + wide)
    large = pltpu.CompilerParams(vmem_limit_bytes=12 * MIB + 2 * wide)

    def cost(us):
        return pl.CostEstimate(flops=0, bytes_accessed=int(us * 3000000), transcendentals=0)

    def spread_of(first, who, places, weights):
        return pl.pallas_call(
            functools.partial(spread_kernel, bits, nb, first),
            out_shape=jax.ShapeDtypeStruct((3 * half, sensors), BF16),
            in_specs=[SMEM_SPEC, VMEM_SPEC, VMEM_SPEC],
            out_specs=VMEM_SPEC,
            compiler_params=small,
            name="spread",
            cost_estimate=cost(1.0),
        )(who, places, weights)

    def exchange(value, bit):
        return lax.ppermute(value, AXES, [(i, i ^ (1 << bit)) for i in range(devices)])

    far_state = pltpu.with_memory_space_constraint(state, pltpu.HBM)
    staging = [pltpu.VMEM((bins, members, cells), F32), pltpu.SemaphoreType.DMA((bins,))]
    piece = pl.pallas_call(
        means_kernel,
        out_shape=jax.ShapeDtypeStruct((nb, rows), F32),
        in_specs=[HBM_SPEC, VMEM_SPEC],
        out_specs=VMEM_SPEC,
        scratch_shapes=staging,
        compiler_params=small,
        name="means",
    )(far_state, kernel.reshape(1, cells))

    who, places, weights = me.reshape(1), blocks.T, foot_weight.T
    orders = batch_order.reshape(batches, P_SIZE)
    own = lax.dynamic_slice_in_dim(orders, me * share, share, 1).reshape(1, batches * share)
    inverse = obs_var.reshape(sensors // 128, 128)

    def roles_of(orders, own, inverse):
        return pl.pallas_call(
            roles_kernel,
            out_shape=[
                jax.ShapeDtypeStruct((batches, sensors), F32),
                jax.ShapeDtypeStruct((sensors, batches * share), BF16),
            ],
            in_specs=[VMEM_SPEC] * 3,
            out_specs=[VMEM_SPEC] * 2,
            compiler_params=small,
            name="roles",
            cost_estimate=cost(0.6),
        )(orders, own, inverse)

    def halves_of(far_state):
        return pl.pallas_call(
            halves_kernel,
            out_shape=jax.ShapeDtypeStruct((bins, 3 * members, cells), BF16),
            in_specs=[HBM_SPEC],
            out_specs=VMEM_SPEC,
            scratch_shapes=staging,
            compiler_params=small,
            name="halves",
            cost_estimate=cost(1.5),
        )(pltpu.with_memory_space_constraint(far_state, pltpu.HBM))

    beside = [
        (functools.partial(spread_of, 0), (who, places, weights)),
        (functools.partial(spread_of, half), (who, places, weights)),
        (roles_of, (orders, own, inverse)),
        (halves_of, (state,)),
    ]
    made = []
    for i, bit in enumerate(bits[:-1]):
        if i < len(beside):
            work, needs = beside[i]
            piece, needs = lax.optimization_barrier((piece, needs))
            other = exchange(piece, bit)
            result = work(*needs)
            other, result = lax.optimization_barrier((other, result))
            made.append(result)
        else:
            other = exchange(piece, bit)
        piece = jnp.concatenate([piece, other], axis=0)
    spread_near, spread_far, (weight, pick), parts = made
    other = exchange(piece, bits[-1])

    left = pltpu.VMEM((rows, 3 * half), BF16)
    resp = bin_response.T
    hx = pl.pallas_call(
        functools.partial(partial_kernel, members, bins),
        out_shape=jax.ShapeDtypeStruct((members, sensors), F32),
        in_specs=[VMEM_SPEC] * 3,
        out_specs=VMEM_SPEC,
        scratch_shapes=[left],
        compiler_params=large,
        name="partial",
        cost_estimate=cost(1.2),
    )(piece, spread_near, resp)

    field, finals = pl.pallas_call(
        functools.partial(update_kernel, members, bins),
        out_shape=[
            jax.ShapeDtypeStruct((members, bins, cells), F32),
            jax.ShapeDtypeStruct((batches * share, members), F32),
        ],
        in_specs=[VMEM_SPEC] * 8,
        out_specs=[HBM_SPEC, VMEM_SPEC],
        scratch_shapes=[
            left,
            pltpu.VMEM((bins, members, cells), F32),
            pltpu.SemaphoreType.DMA((bins,)),
        ],
        compiler_params=large,
        name="update",
    )(hx, other, spread_far, resp, observed.T, weight, pick, parts)
    return (field, finals.reshape(batches, share, members).transpose(0, 2, 1))


def solution(mesh):
    return jax.shard_map(
        shards,
        mesh=mesh,
        in_specs=(
            P(None, None, AXES),
            P(AXES),
            P(),
            P(),
            P(),
            P(),
            P(),
            P(),
        ),
        out_specs=(P(None, None, AXES), P(None, None, AXES)),
        check_vma=False,
    )
```

```python
import functools

import jax
import jax.numpy as jnp
from jax import lax
from jax.experimental import pallas as pl
from jax.experimental.pallas import tpu as pltpu
from jax.sharding import PartitionSpec as P

BLK = 128
P_SIZE = 1024
AXES = ("zrow", "zcol")
F32 = jnp.float32
BF16 = jnp.bfloat16
NT = (((1,), (1,)), ((), ()))
VMEM_SPEC = pl.BlockSpec(memory_space=pltpu.VMEM)
HBM_SPEC = pl.BlockSpec(memory_space=pltpu.HBM)
SMEM_SPEC = pl.BlockSpec(memory_space=pltpu.SMEM)
MIB = 1024 * 1024


def split(x):
    hi = x.astype(BF16)
    return hi, (x - hi.astype(F32)).astype(BF16)


def mm(a, b):
    return jnp.dot(a, b, precision=lax.Precision.HIGHEST, preferred_element_type=F32)


def sublane_mean(x):
    return jnp.sum(x, axis=0, keepdims=True) * (1.0 / x.shape[0])


def lane_mean(x):
    return jnp.sum(x, axis=1, keepdims=True) * (1.0 / x.shape[1])


def means_kernel(x_ref, kernel_ref, out_ref, held_ref, sems, weight_ref, sem):
    members, bins, _ = x_ref.shape
    nb = out_ref.shape[0]
    kernel_copy = pltpu.make_async_copy(kernel_ref, weight_ref, sem)
    kernel_copy.start()
    copies = []
    for b in range(bins):
        copies.append(pltpu.make_async_copy(x_ref.at[:, b, :], held_ref.at[b], sems.at[b]))
        copies[-1].start()
    kernel_copy.wait()
    scale = weight_ref[...] * (1.0 / BLK)
    lane = lax.broadcasted_iota(jnp.int32, (2 * members, 128), 1)
    for b in range(0, bins, 2):
        copies[b].wait()
        copies[b + 1].wait()
        total = jnp.zeros((2 * members, 128), F32)
        for j in range(nb):
            cut = slice(j * BLK, (j + 1) * BLK)
            x = jnp.concatenate([held_ref[b, :, cut], held_ref[b + 1, :, cut]], axis=0)
            summed = jnp.sum(x * scale[:, cut], axis=1, keepdims=True)
            total = jnp.where(lane == j, summed, total)
        out_ref[:, b * members : (b + 2) * members] = total.T[0:nb, :]


def spread_kernel(bits, nb, first, me_ref, blocks_ref, weight_ref, out_ref):
    foot, sensors = blocks_ref.shape
    half = out_ref.shape[0] // 3
    step = 128
    for c in range(0, sensors, step):
        blk = blocks_ref[:, c : c + step]
        away = lax.shift_right_logical(blk, nb.bit_length() - 1) ^ me_ref[0]
        place = blk & (nb - 1)
        for i, bit in enumerate(bits):
            place += (lax.shift_right_logical(away, bit) & 1) * (nb << i)
        weight = weight_ref[:, c : c + step]
        for r in range(0, half, 128):
            row = lax.broadcasted_iota(jnp.int32, (128, step), 0) + (r + first)
            total = jnp.where(row == place[0:1, :], weight[0:1, :], 0.0)
            for f in range(1, foot):
                total += jnp.where(row == place[f : f + 1, :], weight[f : f + 1, :], 0.0)
            hi, low = split(total)
            out_ref[r : r + 128, c : c + step] = hi
            out_ref[half + r : half + r + 128, c : c + step] = low
            out_ref[2 * half + r : 2 * half + r + 128, c : c + step] = hi


def halves_kernel(x_ref, out_ref, held_ref, sems):
    members, bins, _ = x_ref.shape
    copies = []
    for b in range(bins):
        copies.append(pltpu.make_async_copy(x_ref.at[:, b, :], held_ref.at[b], sems.at[b]))
        copies[-1].start()
    for b in range(bins):
        copies[b].wait()
        hi, low = split(held_ref[b])
        out_ref[b, 0:members, :] = hi
        out_ref[b, members : 2 * members, :] = low
        out_ref[b, 2 * members : 3 * members, :] = hi


def roles_kernel(orders_ref, own_ref, var_ref, weight_ref, pick_ref):
    batches, per = orders_ref.shape
    groups = var_ref.shape[0]
    inverse = 1.0 / var_ref[...]
    high = lax.broadcasted_iota(jnp.int32, (groups, per), 0)
    low = lax.broadcasted_iota(jnp.int32, (128, per), 0)
    for t in range(batches):
        order = orders_ref[t : t + 1, :]
        of_high = jnp.where(high == lax.shift_right_logical(order, 7), 1.0, 0.0).astype(BF16)
        of_low = jnp.where(low == (order & 127), 1.0, 0.0).astype(BF16)
        held = lax.dot_general(of_high, of_low, NT, preferred_element_type=F32) * inverse
        for g in range(groups):
            weight_ref[t : t + 1, g * 128 : (g + 1) * 128] = held[g : g + 1, :]
    sensors, nown = pick_ref.shape
    sensor = lax.broadcasted_iota(jnp.int32, (sensors, nown), 0)
    pick_ref[...] = jnp.where(sensor == own_ref[...], 1.0, 0.0).astype(BF16)


def turn(gathered_ref, left):
    half = gathered_ref.shape[0]
    for r in range(0, half, 128):
        hi, low = split(gathered_ref[r : r + 128, :].T)
        left[:, r : r + 128] = hi
        left[:, half + r : half + r + 128] = hi
        left[:, 2 * half + r : 2 * half + r + 128] = low


def observe(members, bins, left, spread_ref, resp_ref, cut):
    z = jnp.dot(left[...], spread_ref[:, cut], preferred_element_type=F32)
    hx = z[0:members, :] * resp_ref[0:1, cut]
    for b in range(1, bins):
        hx += z[b * members : (b + 1) * members, :] * resp_ref[b : b + 1, cut]
    return hx


def partial_kernel(members, bins, gathered_ref, spread_ref, resp_ref, hx_ref, left):
    turn(gathered_ref, left)
    step = 256
    for c in range(0, resp_ref.shape[1], step):
        cut = slice(c, c + step)
        hx_ref[:, cut] = observe(members, bins, left, spread_ref, resp_ref, cut)


def solve(aug):
    n = aug.shape[0]
    width = aug.shape[1]
    rows = [aug[8 * i : 8 * i + 8, :] for i in range(n // 8)]
    sub = lax.broadcasted_iota(jnp.int32, (8, width), 0)

    def lanes(x, j):
        return jnp.broadcast_to(x[:, j : j + 1], (8, width))

    for k in range(n // 8):
        piv = rows[k]
        own = [lanes(piv, 8 * k + q) for q in range(8)]
        for q in range(8):
            here = sub == q
            mult = own[q]
            inv = 1.0 / mult[q : q + 1, :]
            scaled = piv[q : q + 1, :] * inv
            piv = jnp.where(here, scaled, piv - mult * scaled)
            for p in range(q + 1, 8):
                scaled = own[p][q : q + 1, :] * inv
                own[p] = jnp.where(here, scaled, own[p] - mult * scaled)
        for i in range(n // 8):
            if i != k:
                new = rows[i]
                for q in range(8):
                    new = new - lanes(rows[i], 8 * k + q) * piv[q : q + 1, :]
                rows[i] = new
        rows[k] = piv
    return jnp.concatenate(rows, axis=0)[:, n:]


def update_kernel(
    members, bins, hx_ref, gathered_ref, spread_ref, resp_ref, obs_ref, weight_ref, pick_ref, x_ref,
    field_ref, finals_ref, left, out, sems,
):
    sensors = resp_ref.shape[1]
    turn(gathered_ref, left)
    step = 256
    sums = jnp.zeros((2 * members, 2 * members), F32)
    picked = jnp.zeros((2 * members, pick_ref.shape[1]), F32)
    for c in range(0, sensors, step):
        cut = slice(c, c + step)
        hx = hx_ref[:, cut] + observe(members, bins, left, spread_ref, resp_ref, cut)
        center = sublane_mean(hx)
        anom = hx - center
        right = jnp.concatenate([anom, obs_ref[:, cut] - center], axis=0)
        wide = jnp.concatenate([anom * weight_ref[t : t + 1, cut] for t in range(2)], axis=0)
        rhi, rlo = split(right)
        whi, wlo = split(wide)
        sums += lax.dot_general(
            jnp.concatenate([whi, whi, wlo], axis=1),
            jnp.concatenate([rhi, rlo, rhi], axis=1),
            NT,
            preferred_element_type=F32,
        )
        hhi, hlo = split(hx)
        picked += jnp.dot(
            jnp.concatenate([hhi, hlo], axis=0), pick_ref[cut, :], preferred_element_type=F32
        )
    picked = picked[0:members] + picked[members:]
    r64 = lax.broadcasted_iota(jnp.int32, (members, members), 0)
    c64 = lax.broadcasted_iota(jnp.int32, (members, members), 1)
    eye = (r64 == c64).astype(F32)
    s0, e0 = sums[0:members, 0:members], sums[0:members, members:]
    s1, e1 = sums[members:, 0:members], sums[members:, members:]
    gain = solve(jnp.concatenate([s0 + (members - 1.0) * eye, e0 - s0], axis=1))
    first_t = eye + gain - sublane_mean(gain)
    first_ct = first_t - lane_mean(first_t)
    first = first_t.T
    first_c = first - sublane_mean(first)
    prod = mm(s1, jnp.concatenate([first_ct, first_t], axis=1))
    aug = mm(first_c, jnp.concatenate([prod[:, 0:members], e1 - prod[:, members:]], axis=1))
    gain = solve(
        jnp.concatenate([aug[:, 0:members] + (members - 1.0) * eye, aug[:, members:]], axis=1)
    )
    total = first + mm(gain.T, first_c)
    thi, tlo = split(total)
    both = jnp.concatenate([thi, thi, tlo], axis=1)
    copies = []
    for b in range(bins):
        out[b] = jnp.dot(both, x_ref[b], preferred_element_type=F32)
        copies.append(pltpu.make_async_copy(out.at[b], field_ref.at[:, b, :], sems.at[b]))
        copies[-1].start()
    finals_ref[...] = mm(total, picked).T
    for copy in copies:
        copy.wait()


def shards(state, kernel, blocks, foot_weight, bin_response, observed, obs_var, batch_order):
    members, bins, cells = state.shape
    nb = cells // BLK
    sensors = obs_var.shape[0]
    batches = sensors // P_SIZE
    nz, nc = lax.axis_size("zrow"), lax.axis_size("zcol")
    devices = nz * nc
    me = lax.axis_index(AXES)
    share = P_SIZE // devices
    zbits = [(nc << i).bit_length() - 1 for i in range(nz.bit_length() - 1)]
    cbits = [i for i in reversed(range(nc.bit_length() - 1))]
    rounds = [[bit] for bit in reversed(zbits)]
    plane = [bit for bit in cbits if bit > 0]
    while plane:
        rounds.append(sorted(plane[-2:]))
        plane = plane[:-2]
    bits = [bit for group in rounds for bit in group] + [0]
    rows = members * bins
    half = nb * devices // 2
    wide = 6 * half * sensors
    small = pltpu.CompilerParams(vmem_limit_bytes=8 * MIB + wide)
    large = pltpu.CompilerParams(vmem_limit_bytes=12 * MIB + 2 * wide)

    def cost(us):
        return pl.CostEstimate(flops=0, bytes_accessed=int(us * 3000000), transcendentals=0)

    def spread_of(first, who, places, weights):
        return pl.pallas_call(
            functools.partial(spread_kernel, bits, nb, first),
            out_shape=jax.ShapeDtypeStruct((3 * half, sensors), BF16),
            in_specs=[SMEM_SPEC, VMEM_SPEC, VMEM_SPEC],
            out_specs=VMEM_SPEC,
            compiler_params=small,
            name="spread",
            cost_estimate=cost(1.0),
        )(who, places, weights)

    def exchange(value, mask):
        return lax.ppermute(value, AXES, [(i, i ^ mask) for i in range(devices)])

    far_state = pltpu.with_memory_space_constraint(state, pltpu.HBM)
    staging = [pltpu.VMEM((bins, members, cells), F32), pltpu.SemaphoreType.DMA((bins,))]
    piece = pl.pallas_call(
        means_kernel,
        out_shape=jax.ShapeDtypeStruct((nb, rows), F32),
        in_specs=[HBM_SPEC, HBM_SPEC],
        out_specs=VMEM_SPEC,
        scratch_shapes=staging + [pltpu.VMEM((1, cells), F32), pltpu.SemaphoreType.DMA],
        compiler_params=small,
        name="means",
    )(far_state, pltpu.with_memory_space_constraint(kernel.reshape(1, cells), pltpu.HBM))

    who, places, weights = me.reshape(1), blocks.T, foot_weight.T
    orders = batch_order.reshape(batches, P_SIZE)
    own = lax.dynamic_slice_in_dim(orders, me * share, share, 1).reshape(1, batches * share)
    inverse = obs_var.reshape(sensors // 128, 128)

    def roles_of(orders, own, inverse):
        return pl.pallas_call(
            roles_kernel,
            out_shape=[
                jax.ShapeDtypeStruct((batches, sensors), F32),
                jax.ShapeDtypeStruct((sensors, batches * share), BF16),
            ],
            in_specs=[VMEM_SPEC] * 3,
            out_specs=[VMEM_SPEC] * 2,
            compiler_params=small,
            name="roles",
            cost_estimate=cost(0.6),
        )(orders, own, inverse)

    def halves_of(far_state):
        return pl.pallas_call(
            halves_kernel,
            out_shape=jax.ShapeDtypeStruct((bins, 3 * members, cells), BF16),
            in_specs=[HBM_SPEC],
            out_specs=VMEM_SPEC,
            scratch_shapes=staging,
            compiler_params=small,
            name="halves",
            cost_estimate=cost(1.5),
        )(pltpu.with_memory_space_constraint(far_state, pltpu.HBM))

    beside = [
        [(functools.partial(spread_of, 0), (who, places, weights))],
        [(functools.partial(spread_of, half), (who, places, weights))],
        [(roles_of, (orders, own, inverse)), (halves_of, (state,))],
    ]
    made = []
    for i, group in enumerate(rounds):
        work = beside[i] if i < len(beside) else []
        needs = [args for _, args in work]
        piece, needs = lax.optimization_barrier((piece, needs))
        masks = [1 << bit for bit in group]
        if len(masks) == 2:
            masks.append(masks[0] | masks[1])
        others = [exchange(piece, mask) for mask in masks]
        results = [run(*args) for (run, _), args in zip(work, needs)]
        others, results = lax.optimization_barrier((others, results))
        made += results
        piece = jnp.concatenate([piece] + others, axis=0)
    spread_near, spread_far, (weight, pick), parts = made
    other = exchange(piece, 1)

    left = pltpu.VMEM((rows, 3 * half), BF16)
    resp = bin_response.T
    hx = pl.pallas_call(
        functools.partial(partial_kernel, members, bins),
        out_shape=jax.ShapeDtypeStruct((members, sensors), F32),
        in_specs=[VMEM_SPEC] * 3,
        out_specs=VMEM_SPEC,
        scratch_shapes=[left],
        compiler_params=large,
        name="partial",
        cost_estimate=cost(1.2),
    )(piece, spread_near, resp)

    field, finals = pl.pallas_call(
        functools.partial(update_kernel, members, bins),
        out_shape=[
            jax.ShapeDtypeStruct((members, bins, cells), F32),
            jax.ShapeDtypeStruct((batches * share, members), F32),
        ],
        in_specs=[VMEM_SPEC] * 8,
        out_specs=[HBM_SPEC, VMEM_SPEC],
        scratch_shapes=[
            left,
            pltpu.VMEM((bins, members, cells), F32),
            pltpu.SemaphoreType.DMA((bins,)),
        ],
        compiler_params=large,
        name="update",
    )(hx, other, spread_far, resp, observed.T, weight, pick, parts)
    return (field, finals.reshape(batches, share, members).transpose(0, 2, 1))


def solution(mesh):
    return jax.shard_map(
        shards,
        mesh=mesh,
        in_specs=(
            P(None, None, AXES),
            P(AXES),
            P(),
            P(),
            P(),
            P(),
            P(),
            P(),
        ),
        out_specs=(P(None, None, AXES), P(None, None, AXES)),
        check_vma=False,
    )
```

```python
import functools

import jax
import jax.numpy as jnp
from jax import lax
from jax.experimental import pallas as pl
from jax.experimental.pallas import tpu as pltpu
from jax.sharding import PartitionSpec as P

BLK = 128
P_SIZE = 1024
AXES = ("zrow", "zcol")
F32 = jnp.float32
BF16 = jnp.bfloat16
NT = (((1,), (1,)), ((), ()))
VMEM_SPEC = pl.BlockSpec(memory_space=pltpu.VMEM)
HBM_SPEC = pl.BlockSpec(memory_space=pltpu.HBM)
SMEM_SPEC = pl.BlockSpec(memory_space=pltpu.SMEM)
MIB = 1024 * 1024


def split(x):
    hi = x.astype(BF16)
    return hi, (x - hi.astype(F32)).astype(BF16)


def mm(a, b):
    return jnp.dot(a, b, precision=lax.Precision.HIGHEST, preferred_element_type=F32)


def sublane_mean(x):
    return jnp.sum(x, axis=0, keepdims=True) * (1.0 / x.shape[0])


def lane_mean(x):
    return jnp.sum(x, axis=1, keepdims=True) * (1.0 / x.shape[1])


def means_kernel(x_ref, kernel_ref, out_ref, held_ref, sems, weight_ref, sem):
    members, bins, _ = x_ref.shape
    nb = out_ref.shape[0]
    kernel_copy = pltpu.make_async_copy(kernel_ref, weight_ref, sem)
    kernel_copy.start()
    copies = []
    for b in range(bins):
        copies.append(pltpu.make_async_copy(x_ref.at[:, b, :], held_ref.at[b], sems.at[b]))
        copies[-1].start()
    kernel_copy.wait()
    scale = weight_ref[...] * (1.0 / BLK)
    lane = lax.broadcasted_iota(jnp.int32, (2 * members, 128), 1)
    for b in range(0, bins, 2):
        copies[b].wait()
        copies[b + 1].wait()
        total = jnp.zeros((2 * members, 128), F32)
        for j in range(nb):
            cut = slice(j * BLK, (j + 1) * BLK)
            x = jnp.concatenate([held_ref[b, :, cut], held_ref[b + 1, :, cut]], axis=0)
            summed = jnp.sum(x * scale[:, cut], axis=1, keepdims=True)
            total = jnp.where(lane == j, summed, total)
        out_ref[:, b * members : (b + 2) * members] = total.T[0:nb, :]


def spread_kernel(bits, nb, first, me_ref, blocks_ref, weight_ref, out_ref):
    foot, sensors = blocks_ref.shape
    half = out_ref.shape[0] // 3
    step = 128
    for c in range(0, sensors, step):
        blk = blocks_ref[:, c : c + step]
        away = lax.shift_right_logical(blk, nb.bit_length() - 1) ^ me_ref[0]
        place = blk & (nb - 1)
        for i, bit in enumerate(bits):
            place += (lax.shift_right_logical(away, bit) & 1) * (nb << i)
        weight = weight_ref[:, c : c + step]
        for r in range(0, half, 128):
            row = lax.broadcasted_iota(jnp.int32, (128, step), 0) + (r + first)
            total = jnp.where(row == place[0:1, :], weight[0:1, :], 0.0)
            for f in range(1, foot):
                total += jnp.where(row == place[f : f + 1, :], weight[f : f + 1, :], 0.0)
            hi, low = split(total)
            out_ref[r : r + 128, c : c + step] = hi
            out_ref[half + r : half + r + 128, c : c + step] = low
            out_ref[2 * half + r : 2 * half + r + 128, c : c + step] = hi


def halves_kernel(x_ref, out_ref, held_ref, sems):
    members, bins, _ = x_ref.shape
    copies = []
    for b in range(bins):
        copies.append(pltpu.make_async_copy(x_ref.at[:, b, :], held_ref.at[b], sems.at[b]))
        copies[-1].start()
    for b in range(bins):
        copies[b].wait()
        hi, low = split(held_ref[b])
        out_ref[b, 0:members, :] = hi
        out_ref[b, members : 2 * members, :] = low
        out_ref[b, 2 * members : 3 * members, :] = hi


def roles_kernel(orders_ref, own_ref, var_ref, blocks_ref, foot_ref, resp_ref, weight_ref, *table_refs):
    batches, per = orders_ref.shape
    groups = var_ref.shape[0]
    sensors = blocks_ref.shape[1]
    inverse = 1.0 / var_ref[...]
    high = lax.broadcasted_iota(jnp.int32, (groups, per), 0)
    low = lax.broadcasted_iota(jnp.int32, (128, per), 0)
    for t in range(batches):
        order = orders_ref[t : t + 1, :]
        of_high = jnp.where(high == lax.shift_right_logical(order, 7), 1.0, 0.0).astype(BF16)
        of_low = jnp.where(low == (order & 127), 1.0, 0.0).astype(BF16)
        held = lax.dot_general(of_high, of_low, NT, preferred_element_type=F32) * inverse
        for g in range(groups):
            weight_ref[t : t + 1, g * 128 : (g + 1) * 128] = held[g : g + 1, :]
    sensor = lax.broadcasted_iota(jnp.int32, (sensors, 128), 0)
    pick = jnp.where(sensor == own_ref[...], 1.0, 0.0).astype(BF16)
    tables = jnp.concatenate(
        [blocks_ref[...].astype(F32), foot_ref[...], resp_ref[...]], axis=0
    )
    first = tables.astype(BF16)
    rest = tables - first.astype(F32)
    second = rest.astype(BF16)
    third = (rest - second.astype(F32)).astype(BF16)
    stacked = jnp.dot(
        jnp.concatenate([first, second, third], axis=0), pick, preferred_element_type=F32
    )
    n = tables.shape[0]
    own = stacked[0:n] + stacked[n : 2 * n] + stacked[2 * n : 3 * n]
    at = 0
    for ref, table in zip(table_refs, (blocks_ref, foot_ref, resp_ref)):
        rows = table.shape[0]
        ref[:, 0:sensors] = table[...]
        ref[:, sensors : sensors + 128] = own[at : at + rows].astype(ref.dtype)
        at += rows


def obs_kernel(obs_ref, out_ref):
    step = 128
    for c in range(0, obs_ref.shape[1], step):
        hi, low = split(obs_ref[:, c : c + step].T)
        out_ref[0, c : c + step, :] = hi
        out_ref[1, c : c + step, :] = low


def turn(gathered_ref, left):
    half = gathered_ref.shape[0]
    for r in range(0, half, 128):
        hi, low = split(gathered_ref[r : r + 128, :].T)
        left[:, r : r + 128] = hi
        left[:, half + r : half + r + 128] = hi
        left[:, 2 * half + r : 2 * half + r + 128] = low


def observe(members, bins, left, spread_ref, resp_ref, cut):
    z = jnp.dot(left[...], spread_ref[:, cut], preferred_element_type=F32)
    hx = z[0:members, :] * resp_ref[0:1, cut]
    for b in range(1, bins):
        hx += z[b * members : (b + 1) * members, :] * resp_ref[b : b + 1, cut]
    return hx


def partial_kernel(members, bins, gathered_ref, spread_ref, resp_ref, hx_ref, left):
    turn(gathered_ref, left)
    width = resp_ref.shape[1]
    for c in range(0, width, 512):
        cut = slice(c, min(c + 512, width))
        hx_ref[:, cut] = observe(members, bins, left, spread_ref, resp_ref, cut)


def solve(aug):
    n = aug.shape[0]
    width = aug.shape[1]
    rows = [aug[8 * i : 8 * i + 8, :] for i in range(n // 8)]
    sub = lax.broadcasted_iota(jnp.int32, (8, width), 0)

    def lanes(x, j):
        return jnp.broadcast_to(x[:, j : j + 1], (8, width))

    for k in range(n // 8):
        piv = rows[k]
        own = [lanes(piv, 8 * k + q) for q in range(8)]
        for q in range(8):
            here = sub == q
            mult = own[q]
            inv = 1.0 / mult[q : q + 1, :]
            scaled = piv[q : q + 1, :] * inv
            piv = jnp.where(here, scaled, piv - mult * scaled)
            for p in range(q + 1, 8):
                scaled = own[p][q : q + 1, :] * inv
                own[p] = jnp.where(here, scaled, own[p] - mult * scaled)
        for i in range(n // 8):
            if i != k:
                new = rows[i]
                for q in range(8):
                    new = new - lanes(rows[i], 8 * k + q) * piv[q : q + 1, :]
                rows[i] = new
        rows[k] = piv
    return jnp.concatenate(rows, axis=0)[:, n:]


def update_kernel(
    members, bins, hx_ref, gathered_ref, spread_ref, resp_ref, obs_ref, weight_ref, x_ref,
    field_ref, finals_ref, left, anom, out, sems,
):
    sensors = weight_ref.shape[1]
    turn(gathered_ref, left)
    step = 512
    for c in range(0, sensors, step):
        cut = slice(c, c + step)
        hx = hx_ref[:, cut] + observe(members, bins, left, spread_ref, resp_ref, cut)
        center = sublane_mean(hx)
        anom[0:members, cut] = hx - center
        anom[members:, cut] = jnp.broadcast_to(center, (anom.shape[0] - members, step))
    cut = slice(sensors, sensors + 128)
    picked = hx_ref[:, cut] + observe(members, bins, left, spread_ref, resp_ref, cut)
    rhi, rlo = split(anom[...])
    whi, wlo = split(
        jnp.concatenate([anom[0:members, :] * weight_ref[t : t + 1, :] for t in range(2)], axis=0)
    )
    sums = (
        lax.dot_general(whi, rhi, NT, preferred_element_type=F32)
        + lax.dot_general(wlo, rhi, NT, preferred_element_type=F32)
        + lax.dot_general(whi, rlo, NT, preferred_element_type=F32)
    )
    pulls = (
        jnp.dot(whi, obs_ref[0], preferred_element_type=F32)
        + jnp.dot(wlo, obs_ref[0], preferred_element_type=F32)
        + jnp.dot(whi, obs_ref[1], preferred_element_type=F32)
        - sums[:, members : members + 1]
    )
    r64 = lax.broadcasted_iota(jnp.int32, (members, members), 0)
    c64 = lax.broadcasted_iota(jnp.int32, (members, members), 1)
    eye = (r64 == c64).astype(F32)
    s0, e0 = sums[0:members, 0:members], pulls[0:members]
    s1, e1 = sums[members:, 0:members], pulls[members:]
    gain = solve(jnp.concatenate([s0 + (members - 1.0) * eye, e0 - s0], axis=1))
    first_t = eye + gain - sublane_mean(gain)
    first_ct = first_t - lane_mean(first_t)
    first = first_t.T
    first_c = first - sublane_mean(first)
    prod = mm(s1, jnp.concatenate([first_ct, first_t], axis=1))
    aug = mm(first_c, jnp.concatenate([prod[:, 0:members], e1 - prod[:, members:]], axis=1))
    gain = solve(
        jnp.concatenate([aug[:, 0:members] + (members - 1.0) * eye, aug[:, members:]], axis=1)
    )
    total = first + mm(gain.T, first_c)
    thi, tlo = split(total)
    lhs = jnp.concatenate([thi, thi, tlo], axis=1)
    copies = []
    for b in range(bins):
        out[b] = jnp.dot(lhs, x_ref[b], preferred_element_type=F32)
        copies.append(pltpu.make_async_copy(out.at[b], field_ref.at[:, b, :], sems.at[b]))
        copies[-1].start()
    finals_ref[...] = mm(total, picked).T[0 : finals_ref.shape[0], :]
    for copy in copies:
        copy.wait()


def shards(state, kernel, blocks, foot_weight, bin_response, observed, obs_var, batch_order):
    members, bins, cells = state.shape
    nb = cells // BLK
    sensors = obs_var.shape[0]
    batches = sensors // P_SIZE
    nz, nc = lax.axis_size("zrow"), lax.axis_size("zcol")
    devices = nz * nc
    me = lax.axis_index(AXES)
    share = P_SIZE // devices
    zbits = [(nc << i).bit_length() - 1 for i in range(nz.bit_length() - 1)]
    cbits = [i for i in reversed(range(nc.bit_length() - 1))]
    rounds = [[bit] for bit in reversed(zbits)]
    plane = [bit for bit in cbits if bit > 0]
    while plane:
        rounds.append(sorted(plane[-2:]))
        plane = plane[:-2]
    bits = [bit for group in rounds for bit in group] + [0]
    rows = members * bins
    half = nb * devices // 2
    wide = 6 * half * sensors
    width = sensors + 128
    small = pltpu.CompilerParams(vmem_limit_bytes=8 * MIB + wide)
    large = pltpu.CompilerParams(vmem_limit_bytes=12 * MIB + 2 * wide)

    def cost(us):
        return pl.CostEstimate(flops=0, bytes_accessed=int(us * 3000000), transcendentals=0)

    def spread_of(first, who, places, weights):
        return pl.pallas_call(
            functools.partial(spread_kernel, bits, nb, first),
            out_shape=jax.ShapeDtypeStruct((3 * half, width), BF16),
            in_specs=[SMEM_SPEC, VMEM_SPEC, VMEM_SPEC],
            out_specs=VMEM_SPEC,
            compiler_params=small,
            name="spread",
            cost_estimate=cost(1.0),
        )(who, places, weights)

    def exchange(value, mask):
        return lax.ppermute(value, AXES, [(i, i ^ mask) for i in range(devices)])

    far_state = pltpu.with_memory_space_constraint(state, pltpu.HBM)
    staging = [pltpu.VMEM((bins, members, cells), F32), pltpu.SemaphoreType.DMA((bins,))]
    piece = pl.pallas_call(
        means_kernel,
        out_shape=jax.ShapeDtypeStruct((nb, rows), F32),
        in_specs=[HBM_SPEC, HBM_SPEC],
        out_specs=VMEM_SPEC,
        scratch_shapes=staging + [pltpu.VMEM((1, cells), F32), pltpu.SemaphoreType.DMA],
        compiler_params=small,
        name="means",
    )(far_state, pltpu.with_memory_space_constraint(kernel.reshape(1, cells), pltpu.HBM))

    who, places, weights = me.reshape(1), blocks.T, foot_weight.T
    orders = batch_order.reshape(batches, P_SIZE)
    inverse = obs_var.reshape(sensors // 128, 128)

    def roles_of(*args):
        return pl.pallas_call(
            roles_kernel,
            out_shape=[
                jax.ShapeDtypeStruct((batches, sensors), F32),
                jax.ShapeDtypeStruct((blocks.shape[1], width), jnp.int32),
                jax.ShapeDtypeStruct((blocks.shape[1], width), F32),
                jax.ShapeDtypeStruct((bins, width), F32),
            ],
            in_specs=[VMEM_SPEC] * 6,
            out_specs=[VMEM_SPEC] * 4,
            compiler_params=small,
            name="roles",
            cost_estimate=cost(0.6),
        )(*args)

    def obs_of(observed):
        return pl.pallas_call(
            obs_kernel,
            out_shape=jax.ShapeDtypeStruct((2, sensors, members), BF16),
            in_specs=[VMEM_SPEC],
            out_specs=VMEM_SPEC,
            compiler_params=small,
            name="observed",
            cost_estimate=cost(0.4),
        )(observed)

    def halves_of(far_state):
        return pl.pallas_call(
            halves_kernel,
            out_shape=jax.ShapeDtypeStruct((bins, 3 * members, cells), BF16),
            in_specs=[HBM_SPEC],
            out_specs=VMEM_SPEC,
            scratch_shapes=staging,
            compiler_params=small,
            name="halves",
            cost_estimate=cost(1.5),
        )(pltpu.with_memory_space_constraint(far_state, pltpu.HBM))

    made = {}

    def first_work():
        own = lax.dynamic_slice_in_dim(orders, me * share, share, 1).reshape(1, batches * share)
        own = jnp.pad(own, ((0, 0), (0, 128 - batches * share)), constant_values=-1)
        made["roles"] = roles_of(orders, own, inverse, places, weights, bin_response.T)
        made["near"] = spread_of(0, who, *made["roles"][1:3])

    def second_work():
        made["far"] = spread_of(half, who, *made["roles"][1:3])

    def third_work():
        made["parts"] = halves_of(state)
        made["obs"] = obs_of(observed.T)

    beside = [first_work, second_work, third_work]
    for i, group in enumerate(rounds):
        masks = [1 << bit for bit in group]
        if len(masks) == 2:
            masks.append(masks[0] | masks[1])
        if i == 0:
            piece, orders, places, weights = lax.optimization_barrier(
                (piece, orders, places, weights)
            )
        elif i == 1:
            piece, who = lax.optimization_barrier((piece, who))
        elif i == 2:
            piece, state, observed = lax.optimization_barrier((piece, state, observed))
        others = [exchange(piece, mask) for mask in masks]
        if i < len(beside):
            beside[i]()
        others, made = lax.optimization_barrier((others, made))
        piece = jnp.concatenate([piece] + others, axis=0)
    weight, _, _, resp = made["roles"]
    other = exchange(piece, 1)

    left = pltpu.VMEM((rows, 3 * half), BF16)
    hx = pl.pallas_call(
        functools.partial(partial_kernel, members, bins),
        out_shape=jax.ShapeDtypeStruct((members, width), F32),
        in_specs=[VMEM_SPEC] * 3,
        out_specs=VMEM_SPEC,
        scratch_shapes=[left],
        compiler_params=large,
        name="partial",
        cost_estimate=cost(1.2),
    )(piece, made["near"], resp)

    field, finals = pl.pallas_call(
        functools.partial(update_kernel, members, bins),
        out_shape=[
            jax.ShapeDtypeStruct((members, bins, cells), F32),
            jax.ShapeDtypeStruct((batches * share, members), F32),
        ],
        in_specs=[VMEM_SPEC] * 7,
        out_specs=[HBM_SPEC, VMEM_SPEC],
        scratch_shapes=[
            left,
            pltpu.VMEM((members + 16, sensors), F32),
            pltpu.VMEM((bins, members, cells), F32),
            pltpu.SemaphoreType.DMA((bins,)),
        ],
        compiler_params=large,
        name="update",
    )(hx, other, made["far"], resp, made["obs"], weight, made["parts"])
    return (field, finals.reshape(batches, share, members).transpose(0, 2, 1))


def solution(mesh):
    return jax.shard_map(
        shards,
        mesh=mesh,
        in_specs=(
            P(None, None, AXES),
            P(AXES),
            P(),
            P(),
            P(),
            P(),
            P(),
            P(),
        ),
        out_specs=(P(None, None, AXES), P(None, None, AXES)),
        check_vma=False,
    )
```

```python
import functools

import jax
import jax.numpy as jnp
from jax import lax
from jax.experimental import pallas as pl
from jax.experimental.pallas import tpu as pltpu
from jax.sharding import PartitionSpec as P

BLK = 128
P_SIZE = 1024
AXES = ("zrow", "zcol")
F32 = jnp.float32
BF16 = jnp.bfloat16
NT = (((1,), (1,)), ((), ()))
VMEM_SPEC = pl.BlockSpec(memory_space=pltpu.VMEM)
HBM_SPEC = pl.BlockSpec(memory_space=pltpu.HBM)
SMEM_SPEC = pl.BlockSpec(memory_space=pltpu.SMEM)
MIB = 1024 * 1024


def split(x):
    hi = x.astype(BF16)
    return hi, (x - hi.astype(F32)).astype(BF16)


def mm(a, b):
    return jnp.dot(a, b, precision=lax.Precision.HIGHEST, preferred_element_type=F32)


def sublane_mean(x):
    return jnp.sum(x, axis=0, keepdims=True) * (1.0 / x.shape[0])


def lane_mean(x):
    return jnp.sum(x, axis=1, keepdims=True) * (1.0 / x.shape[1])


def means_kernel(x_ref, kernel_ref, out_ref, held_ref, sems, weight_ref, sem):
    members, bins, _ = x_ref.shape
    nb = out_ref.shape[0]
    kernel_copy = pltpu.make_async_copy(kernel_ref, weight_ref, sem)
    kernel_copy.start()
    copies = []
    for b in range(bins):
        copies.append(pltpu.make_async_copy(x_ref.at[:, b, :], held_ref.at[b], sems.at[b]))
        copies[-1].start()
    kernel_copy.wait()
    scale = weight_ref[...] * (1.0 / BLK)
    lane = lax.broadcasted_iota(jnp.int32, (2 * members, 128), 1)
    for b in range(0, bins, 2):
        copies[b].wait()
        copies[b + 1].wait()
        total = jnp.zeros((2 * members, 128), F32)
        for j in range(nb):
            cut = slice(j * BLK, (j + 1) * BLK)
            x = jnp.concatenate([held_ref[b, :, cut], held_ref[b + 1, :, cut]], axis=0)
            summed = jnp.sum(x * scale[:, cut], axis=1, keepdims=True)
            total = jnp.where(lane == j, summed, total)
        out_ref[:, b * members : (b + 2) * members] = total.T[0:nb, :]


def spread_kernel(bits, nb, first, me_ref, blocks_ref, weight_ref, out_ref):
    foot, sensors = blocks_ref.shape
    half = out_ref.shape[0] // 3
    step = 128
    for c in range(0, sensors, step):
        blk = blocks_ref[:, c : c + step]
        away = lax.shift_right_logical(blk, nb.bit_length() - 1) ^ me_ref[0]
        place = blk & (nb - 1)
        for i, bit in enumerate(bits):
            place += (lax.shift_right_logical(away, bit) & 1) * (nb << i)
        weight = weight_ref[:, c : c + step]
        for r in range(0, half, 128):
            row = lax.broadcasted_iota(jnp.int32, (128, step), 0) + (r + first)
            total = jnp.where(row == place[0:1, :], weight[0:1, :], 0.0)
            for f in range(1, foot):
                total += jnp.where(row == place[f : f + 1, :], weight[f : f + 1, :], 0.0)
            hi, low = split(total)
            out_ref[r : r + 128, c : c + step] = hi
            out_ref[half + r : half + r + 128, c : c + step] = low
            out_ref[2 * half + r : 2 * half + r + 128, c : c + step] = hi


def halves_kernel(x_ref, out_ref, held_ref, sems):
    members, bins, _ = x_ref.shape
    copies = []
    for b in range(bins):
        copies.append(pltpu.make_async_copy(x_ref.at[:, b, :], held_ref.at[b], sems.at[b]))
        copies[-1].start()
    for b in range(bins):
        copies[b].wait()
        hi, low = split(held_ref[b])
        out_ref[b, 0:members, :] = hi
        out_ref[b, members : 2 * members, :] = low
        out_ref[b, 2 * members : 3 * members, :] = hi


def roles_kernel(share, me_ref, orders_ref, var_ref, blocks_ref, foot_ref, resp_ref, weight_ref, *table_refs):
    batches = weight_ref.shape[0]
    groups = var_ref.shape[0]
    each = groups // batches
    per = each * 128
    sensors = blocks_ref.shape[1]
    start = me_ref[0] * share
    lane = lax.broadcasted_iota(jnp.int32, (8, 128), 1)
    own = jnp.full((8, 128), -1, jnp.int32)
    inverse = 1.0 / var_ref[...]
    high = lax.broadcasted_iota(jnp.int32, (groups, per), 0)
    low = lax.broadcasted_iota(jnp.int32, (128, per), 0)
    for t in range(batches):
        order = jnp.concatenate(
            [orders_ref[g : g + 1, :] for g in range(t * each, (t + 1) * each)], axis=1
        )
        mine = orders_ref[pl.ds(t * each + lax.shift_right_logical(start, 7), 1), :]
        mine = pltpu.roll(
            jnp.broadcast_to(mine, (8, 128)), (t * share - (start & 127)) & 127, axis=1
        )
        own = jnp.where((lane >= t * share) & (lane < (t + 1) * share), mine, own)
        of_high = jnp.where(high == lax.shift_right_logical(order, 7), 1.0, 0.0).astype(BF16)
        of_low = jnp.where(low == (order & 127), 1.0, 0.0).astype(BF16)
        held = lax.dot_general(of_high, of_low, NT, preferred_element_type=F32) * inverse
        for g in range(groups):
            weight_ref[t : t + 1, g * 128 : (g + 1) * 128] = held[g : g + 1, :]
    sensor = lax.broadcasted_iota(jnp.int32, (sensors, 128), 0)
    pick = jnp.where(sensor == own[0:1, :], 1.0, 0.0).astype(BF16)
    tables = jnp.concatenate(
        [blocks_ref[...].astype(F32), foot_ref[...], resp_ref[...]], axis=0
    )
    first = tables.astype(BF16)
    rest = tables - first.astype(F32)
    second = rest.astype(BF16)
    third = (rest - second.astype(F32)).astype(BF16)
    stacked = jnp.dot(
        jnp.concatenate([first, second, third], axis=0), pick, preferred_element_type=F32
    )
    n = tables.shape[0]
    chosen = stacked[0:n] + stacked[n : 2 * n] + stacked[2 * n : 3 * n]
    at = 0
    for ref, table in zip(table_refs, (blocks_ref, foot_ref, resp_ref)):
        rows = table.shape[0]
        ref[:, 0:sensors] = table[...]
        ref[:, sensors : sensors + 128] = chosen[at : at + rows].astype(ref.dtype)
        at += rows


def obs_kernel(obs_ref, out_ref):
    members = obs_ref.shape[0]
    step = 128
    for c in range(0, obs_ref.shape[1], step):
        turned = obs_ref[:, c : c + step].T
        hi, low = split(jnp.concatenate([jnp.zeros_like(turned), turned], axis=1))
        out_ref[0, c : c + step, :] = hi
        out_ref[1, c : c + step, :] = low


def turn(gathered_ref, left):
    half = gathered_ref.shape[0]
    for r in range(0, half, 128):
        hi, low = split(gathered_ref[r : r + 128, :].T)
        left[:, r : r + 128] = hi
        left[:, half + r : half + r + 128] = hi
        left[:, 2 * half + r : 2 * half + r + 128] = low


def observe(members, bins, left, spread_ref, resp_ref, cut):
    z = jnp.dot(left[...], spread_ref[:, cut], preferred_element_type=F32)
    hx = z[0:members, :] * resp_ref[0:1, cut]
    for b in range(1, bins):
        hx += z[b * members : (b + 1) * members, :] * resp_ref[b : b + 1, cut]
    return hx


def partial_kernel(members, bins, gathered_ref, spread_ref, resp_ref, hx_ref, left):
    turn(gathered_ref, left)
    width = resp_ref.shape[1]
    for c in range(0, width, 512):
        cut = slice(c, min(c + 512, width))
        hx_ref[:, cut] = observe(members, bins, left, spread_ref, resp_ref, cut)


def solve(aug):
    n, width = aug.shape
    p = 16
    blocks = n // p
    rows = [aug[p * i : p * i + p, :] for i in range(blocks)]
    sub = lax.broadcasted_iota(jnp.int32, (p, width), 0)

    def lanes(x, j):
        return jnp.broadcast_to(x[:, j : j + 1], (p, width))

    for k in range(blocks):
        piv = rows[k]
        own = [lanes(piv, p * k + q) for q in range(p)]
        for q in range(p):
            here = sub == q
            mult = own[q]
            inv = 1.0 / mult[q : q + 1, :]
            scaled = piv[q : q + 1, :] * inv
            piv = jnp.where(here, scaled, piv - mult * scaled)
            for r in range(q + 1, p):
                scaled = own[r][q : q + 1, :] * inv
                own[r] = jnp.where(here, scaled, own[r] - mult * scaled)
        for i in list(range(k + 1, blocks)) + list(range(k)):
            new = rows[i]
            for q in range(p):
                new = new - lanes(rows[i], p * k + q) * piv[q : q + 1, :]
            rows[i] = new
        rows[k] = piv
    return jnp.concatenate(rows, axis=0)


def update_kernel(
    members, bins, hx_ref, gathered_ref, spread_ref, resp_ref, obs_ref, weight_ref, x_ref,
    field_ref, finals_ref, left, anom, out, sems,
):
    sensors = weight_ref.shape[1]
    turn(gathered_ref, left)
    step = 512
    for c in range(0, sensors, step):
        cut = slice(c, c + step)
        hx = hx_ref[:, cut] + observe(members, bins, left, spread_ref, resp_ref, cut)
        center = sublane_mean(hx)
        anom[0:members, cut] = hx - center
        anom[members:, cut] = jnp.broadcast_to(center, (anom.shape[0] - members, step))
    cut = slice(sensors, sensors + 128)
    picked = hx_ref[:, cut] + observe(members, bins, left, spread_ref, resp_ref, cut)
    rhi, rlo = split(anom[...])
    whi, wlo = split(
        jnp.concatenate([anom[0:members, :] * weight_ref[t : t + 1, :] for t in range(2)], axis=0)
    )
    sums = (
        lax.dot_general(whi, rhi, NT, preferred_element_type=F32)
        + lax.dot_general(wlo, rhi, NT, preferred_element_type=F32)
        + lax.dot_general(whi, rlo, NT, preferred_element_type=F32)
    )
    pulls = (
        jnp.dot(whi, obs_ref[0], preferred_element_type=F32)
        + jnp.dot(wlo, obs_ref[0], preferred_element_type=F32)
        + jnp.dot(whi, obs_ref[1], preferred_element_type=F32)
    )
    lane = lax.broadcasted_iota(jnp.int32, (2 * members, 2 * members), 1)
    wide_sums = jnp.concatenate(
        [sums, jnp.zeros((2 * members, 2 * members - sums.shape[1]), F32)], axis=1
    )
    base = jnp.where(lane < members, wide_sums, pulls - sums[:, members : members + 1])
    lane = lane[0:members]
    right = lane >= members
    row = lax.broadcasted_iota(jnp.int32, lane.shape, 0)
    prior = jnp.where((lane == row) | (lane == row + members), members - 1.0, 0.0)
    even = jnp.where(right, 1.0 / members, 0.0)

    def mixer_t(solved):
        held = jnp.where(right, solved, 0.0)
        return held - sublane_mean(held) + even

    first_t = mixer_t(solve(base[0:members] + prior))
    tilt = jnp.sum(first_t, axis=1, keepdims=True) * (1.0 / members)
    first = first_t.T[members:, :]
    first_c = first - sublane_mean(first)
    moved = mm(first_c, base[members:])
    swapped = pltpu.roll(first_t, members, axis=1) - tilt
    crossed = mm(moved[:, 0:members], jnp.where(right, tilt, swapped))
    second_t = mixer_t(
        solve(prior + jnp.where(right, moved - crossed, crossed))
    )
    total = mm(second_t.T[members:, :], jnp.concatenate([first, first], axis=1))
    thi, tlo = split(total)
    lhs = jnp.concatenate([thi, tlo[:, 0:members]], axis=1)
    copies = []
    for b in range(bins):
        out[b] = jnp.dot(lhs, x_ref[b], preferred_element_type=F32)
        copies.append(pltpu.make_async_copy(out.at[b], field_ref.at[:, b, :], sems.at[b]))
        copies[-1].start()
    finals_ref[...] = mm(total[:, 0:members], picked).T[0 : finals_ref.shape[0], :]
    for copy in copies:
        copy.wait()


def shards(state, kernel, blocks, foot_weight, bin_response, observed, obs_var, batch_order):
    members, bins, cells = state.shape
    nb = cells // BLK
    sensors = obs_var.shape[0]
    batches = sensors // P_SIZE
    nz, nc = lax.axis_size("zrow"), lax.axis_size("zcol")
    devices = nz * nc
    me = lax.axis_index(AXES)
    share = P_SIZE // devices
    zbits = [(nc << i).bit_length() - 1 for i in range(nz.bit_length() - 1)]
    cbits = [i for i in reversed(range(nc.bit_length() - 1))]
    rounds = [[bit] for bit in reversed(zbits)]
    plane = [bit for bit in cbits if bit > 0]
    while plane:
        rounds.append(sorted(plane[-2:]))
        plane = plane[:-2]
    bits = [bit for group in rounds for bit in group] + [0]
    rows = members * bins
    half = nb * devices // 2
    wide = 6 * half * sensors
    width = sensors + 128
    small = pltpu.CompilerParams(vmem_limit_bytes=8 * MIB + wide)
    large = pltpu.CompilerParams(vmem_limit_bytes=12 * MIB + 2 * wide)

    def cost(us):
        return pl.CostEstimate(flops=0, bytes_accessed=int(us * 3000000), transcendentals=0)

    def spread_of(first, who, places, weights):
        return pl.pallas_call(
            functools.partial(spread_kernel, bits, nb, first),
            out_shape=jax.ShapeDtypeStruct((3 * half, width), BF16),
            in_specs=[SMEM_SPEC, VMEM_SPEC, VMEM_SPEC],
            out_specs=VMEM_SPEC,
            compiler_params=small,
            name="spread",
            cost_estimate=cost(1.0),
        )(who, places, weights)

    def exchange(value, mask):
        return lax.ppermute(value, AXES, [(i, i ^ mask) for i in range(devices)])

    far_state = pltpu.with_memory_space_constraint(state, pltpu.HBM)
    staging = [pltpu.VMEM((bins, members, cells), F32), pltpu.SemaphoreType.DMA((bins,))]
    piece = pl.pallas_call(
        means_kernel,
        out_shape=jax.ShapeDtypeStruct((nb, rows), F32),
        in_specs=[HBM_SPEC, HBM_SPEC],
        out_specs=VMEM_SPEC,
        scratch_shapes=staging + [pltpu.VMEM((1, cells), F32), pltpu.SemaphoreType.DMA],
        compiler_params=small,
        name="means",
    )(far_state, pltpu.with_memory_space_constraint(kernel.reshape(1, cells), pltpu.HBM))

    who, places, weights = me.reshape(1), blocks.T, foot_weight.T
    orders = batch_order.reshape(sensors // 128, 128)
    inverse = obs_var.reshape(sensors // 128, 128)

    def roles_of(*args):
        return pl.pallas_call(
            functools.partial(roles_kernel, share),
            out_shape=[
                jax.ShapeDtypeStruct((batches, sensors), F32),
                jax.ShapeDtypeStruct((blocks.shape[1], width), jnp.int32),
                jax.ShapeDtypeStruct((blocks.shape[1], width), F32),
                jax.ShapeDtypeStruct((bins, width), F32),
            ],
            in_specs=[SMEM_SPEC] + [VMEM_SPEC] * 5,
            out_specs=[VMEM_SPEC] * 4,
            compiler_params=small,
            name="roles",
            cost_estimate=cost(0.6),
        )(*args)

    def obs_of(observed):
        return pl.pallas_call(
            obs_kernel,
            out_shape=jax.ShapeDtypeStruct((2, sensors, 2 * members), BF16),
            in_specs=[VMEM_SPEC],
            out_specs=VMEM_SPEC,
            compiler_params=small,
            name="observed",
            cost_estimate=cost(0.4),
        )(observed)

    def halves_of(far_state):
        return pl.pallas_call(
            halves_kernel,
            out_shape=jax.ShapeDtypeStruct((bins, 3 * members, cells), BF16),
            in_specs=[HBM_SPEC],
            out_specs=VMEM_SPEC,
            scratch_shapes=staging,
            compiler_params=small,
            name="halves",
            cost_estimate=cost(1.5),
        )(pltpu.with_memory_space_constraint(far_state, pltpu.HBM))

    made = {}

    def first_work():
        made["roles"] = roles_of(who, orders, inverse, places, weights, bin_response.T)
        made["near"] = spread_of(0, who, *made["roles"][1:3])

    def second_work():
        made["far"] = spread_of(half, who, *made["roles"][1:3])

    def third_work():
        made["parts"] = halves_of(state)
        made["obs"] = obs_of(observed.T)

    beside = [first_work, second_work, third_work]
    for i, group in enumerate(rounds):
        masks = [1 << bit for bit in group]
        if len(masks) == 2:
            masks.append(masks[0] | masks[1])
        if i == 0:
            piece, orders, places, weights = lax.optimization_barrier(
                (piece, orders, places, weights)
            )
        elif i == 1:
            piece, who = lax.optimization_barrier((piece, who))
        elif i == 2:
            piece, state, observed = lax.optimization_barrier((piece, state, observed))
        others = [exchange(piece, mask) for mask in masks]
        if i < len(beside):
            beside[i]()
        others, made = lax.optimization_barrier((others, made))
        piece = jnp.concatenate([piece] + others, axis=0)
    weight, _, _, resp = made["roles"]
    other = exchange(piece, 1)

    left = pltpu.VMEM((rows, 3 * half), BF16)
    hx = pl.pallas_call(
        functools.partial(partial_kernel, members, bins),
        out_shape=jax.ShapeDtypeStruct((members, width), F32),
        in_specs=[VMEM_SPEC] * 3,
        out_specs=VMEM_SPEC,
        scratch_shapes=[left],
        compiler_params=large,
        name="partial",
        cost_estimate=cost(1.2),
    )(piece, made["near"], resp)

    field, finals = pl.pallas_call(
        functools.partial(update_kernel, members, bins),
        out_shape=[
            jax.ShapeDtypeStruct((members, bins, cells), F32),
            jax.ShapeDtypeStruct((batches * share, members), F32),
        ],
        in_specs=[VMEM_SPEC] * 7,
        out_specs=[HBM_SPEC, VMEM_SPEC],
        scratch_shapes=[
            left,
            pltpu.VMEM((members + 16, sensors), F32),
            pltpu.VMEM((bins, members, cells), F32),
            pltpu.SemaphoreType.DMA((bins,)),
        ],
        compiler_params=large,
        name="update",
    )(hx, other, made["far"], resp, made["obs"], weight, made["parts"])
    return (field, finals.reshape(batches, share, members).transpose(0, 2, 1))


def solution(mesh):
    return jax.shard_map(
        shards,
        mesh=mesh,
        in_specs=(
            P(None, None, AXES),
            P(AXES),
            P(),
            P(),
            P(),
            P(),
            P(),
            P(),
        ),
        out_specs=(P(None, None, AXES), P(None, None, AXES)),
        check_vma=False,
    )
```

```python
import functools

import jax
import jax.numpy as jnp
from jax import lax
from jax.experimental import pallas as pl
from jax.experimental.pallas import tpu as pltpu
from jax.sharding import PartitionSpec as P

BLK = 128
P_SIZE = 1024
AXES = ("zrow", "zcol")
F32 = jnp.float32
BF16 = jnp.bfloat16
NT = (((1,), (1,)), ((), ()))
VMEM_SPEC = pl.BlockSpec(memory_space=pltpu.VMEM)
HBM_SPEC = pl.BlockSpec(memory_space=pltpu.HBM)
SMEM_SPEC = pl.BlockSpec(memory_space=pltpu.SMEM)
MIB = 1024 * 1024


def split(x):
    hi = x.astype(BF16)
    return hi, (x - hi.astype(F32)).astype(BF16)


def mm(a, b):
    return jnp.dot(a, b, precision=lax.Precision.HIGHEST, preferred_element_type=F32)


def sublane_mean(x):
    return jnp.sum(x, axis=0, keepdims=True) * (1.0 / x.shape[0])


def lane_mean(x):
    return jnp.sum(x, axis=1, keepdims=True) * (1.0 / x.shape[1])


def means_kernel(x_ref, kernel_ref, out_ref, held_ref, sems, weight_ref, sem):
    members, bins, _ = x_ref.shape
    nb = out_ref.shape[0]
    kernel_copy = pltpu.make_async_copy(kernel_ref, weight_ref, sem)
    kernel_copy.start()
    copies = []
    for b in range(bins):
        copies.append(pltpu.make_async_copy(x_ref.at[:, b, :], held_ref.at[b], sems.at[b]))
        copies[-1].start()
    kernel_copy.wait()
    scale = weight_ref[...] * (1.0 / BLK)
    lane = lax.broadcasted_iota(jnp.int32, (2 * members, 128), 1)
    for b in range(0, bins, 2):
        copies[b].wait()
        copies[b + 1].wait()
        total = jnp.zeros((2 * members, 128), F32)
        for j in range(nb):
            cut = slice(j * BLK, (j + 1) * BLK)
            x = jnp.concatenate([held_ref[b, :, cut], held_ref[b + 1, :, cut]], axis=0)
            summed = jnp.sum(x * scale[:, cut], axis=1, keepdims=True)
            total = jnp.where(lane == j, summed, total)
        out_ref[:, b * members : (b + 2) * members] = total.T[0:nb, :]


def spread_kernel(bits, nb, first, me_ref, blocks_ref, weight_ref, out_ref):
    foot, sensors = blocks_ref.shape
    half = out_ref.shape[0] // 3
    step = 128
    for c in range(0, sensors, step):
        blk = blocks_ref[:, c : c + step]
        away = lax.shift_right_logical(blk, nb.bit_length() - 1) ^ me_ref[0]
        place = blk & (nb - 1)
        for i, bit in enumerate(bits):
            place += (lax.shift_right_logical(away, bit) & 1) * (nb << i)
        weight = weight_ref[:, c : c + step]
        for r in range(0, half, 128):
            row = lax.broadcasted_iota(jnp.int32, (128, step), 0) + (r + first)
            total = jnp.where(row == place[0:1, :], weight[0:1, :], 0.0)
            for f in range(1, foot):
                total += jnp.where(row == place[f : f + 1, :], weight[f : f + 1, :], 0.0)
            hi, low = split(total)
            out_ref[r : r + 128, c : c + step] = hi
            out_ref[half + r : half + r + 128, c : c + step] = low
            out_ref[2 * half + r : 2 * half + r + 128, c : c + step] = hi


def halves_kernel(x_ref, out_ref, held_ref, sems):
    members, bins, _ = x_ref.shape
    copies = []
    for b in range(bins):
        copies.append(pltpu.make_async_copy(x_ref.at[:, b, :], held_ref.at[b], sems.at[b]))
        copies[-1].start()
    for b in range(bins):
        copies[b].wait()
        hi, low = split(held_ref[b])
        out_ref[b, 0:members, :] = hi
        out_ref[b, members : 2 * members, :] = low
        out_ref[b, 2 * members : 3 * members, :] = hi


def roles_kernel(share, me_ref, orders_ref, var_ref, blocks_ref, foot_ref, resp_ref, weight_ref, *table_refs):
    batches = weight_ref.shape[0]
    groups = var_ref.shape[0]
    each = groups // batches
    per = each * 128
    sensors = blocks_ref.shape[1]
    start = me_ref[0] * share
    lane = lax.broadcasted_iota(jnp.int32, (8, 128), 1)
    own = jnp.full((8, 128), -1, jnp.int32)
    inverse = 1.0 / var_ref[...]
    high = lax.broadcasted_iota(jnp.int32, (groups, per), 0)
    low = lax.broadcasted_iota(jnp.int32, (128, per), 0)
    for t in range(batches):
        order = jnp.concatenate(
            [orders_ref[g : g + 1, :] for g in range(t * each, (t + 1) * each)], axis=1
        )
        mine = orders_ref[pl.ds(t * each + lax.shift_right_logical(start, 7), 1), :]
        mine = pltpu.roll(
            jnp.broadcast_to(mine, (8, 128)), (t * share - (start & 127)) & 127, axis=1
        )
        own = jnp.where((lane >= t * share) & (lane < (t + 1) * share), mine, own)
        of_high = jnp.where(high == lax.shift_right_logical(order, 7), 1.0, 0.0).astype(BF16)
        of_low = jnp.where(low == (order & 127), 1.0, 0.0).astype(BF16)
        held = lax.dot_general(of_high, of_low, NT, preferred_element_type=F32) * inverse
        for g in range(groups):
            weight_ref[t : t + 1, g * 128 : (g + 1) * 128] = held[g : g + 1, :]
    sensor = lax.broadcasted_iota(jnp.int32, (sensors, 128), 0)
    pick = jnp.where(sensor == own[0:1, :], 1.0, 0.0).astype(BF16)
    tables = jnp.concatenate(
        [blocks_ref[...].astype(F32), foot_ref[...], resp_ref[...]], axis=0
    )
    first = tables.astype(BF16)
    rest = tables - first.astype(F32)
    second = rest.astype(BF16)
    third = (rest - second.astype(F32)).astype(BF16)
    stacked = jnp.dot(
        jnp.concatenate([first, second, third], axis=0), pick, preferred_element_type=F32
    )
    n = tables.shape[0]
    chosen = stacked[0:n] + stacked[n : 2 * n] + stacked[2 * n : 3 * n]
    at = 0
    for ref, table in zip(table_refs, (blocks_ref, foot_ref, resp_ref)):
        rows = table.shape[0]
        ref[:, 0:sensors] = table[...]
        ref[:, sensors : sensors + 128] = chosen[at : at + rows].astype(ref.dtype)
        at += rows


def obs_kernel(obs_ref, out_ref):
    members = obs_ref.shape[0]
    step = 128
    for c in range(0, obs_ref.shape[1], step):
        turned = obs_ref[:, c : c + step].T
        hi, low = split(jnp.concatenate([jnp.zeros_like(turned), turned], axis=1))
        out_ref[0, c : c + step, :] = hi
        out_ref[1, c : c + step, :] = low


def turn(gathered_ref, left):
    half = gathered_ref.shape[0]
    for r in range(0, half, 128):
        hi, low = split(gathered_ref[r : r + 128, :].T)
        left[:, r : r + 128] = hi
        left[:, half + r : half + r + 128] = hi
        left[:, 2 * half + r : 2 * half + r + 128] = low


def observe(members, bins, left, spread_ref, resp_ref, cut):
    z = jnp.dot(left[...], spread_ref[:, cut], preferred_element_type=F32)
    hx = z[0:members, :] * resp_ref[0:1, cut]
    for b in range(1, bins):
        hx += z[b * members : (b + 1) * members, :] * resp_ref[b : b + 1, cut]
    return hx


def partial_kernel(members, bins, gathered_ref, spread_ref, resp_ref, hx_ref, left):
    turn(gathered_ref, left)
    width = resp_ref.shape[1]
    for c in range(0, width, 512):
        cut = slice(c, min(c + 512, width))
        hx_ref[:, cut] = observe(members, bins, left, spread_ref, resp_ref, cut)


def solve(aug):
    n, width = aug.shape
    p = 16
    blocks = n // p
    rows = [aug[p * i : p * i + p, :] for i in range(blocks)]
    sub = lax.broadcasted_iota(jnp.int32, (p, width), 0)

    def lanes(x, j):
        return jnp.broadcast_to(x[:, j : j + 1], (p, width))

    for k in range(blocks):
        piv = rows[k]
        own = [lanes(piv, p * k + q) for q in range(p)]
        for q in range(p):
            here = sub == q
            mult = own[q]
            inv = 1.0 / mult[q : q + 1, :]
            scaled = piv[q : q + 1, :] * inv
            piv = jnp.where(here, scaled, piv - mult * scaled)
            for r in range(q + 1, p):
                scaled = own[r][q : q + 1, :] * inv
                own[r] = jnp.where(here, scaled, own[r] - mult * scaled)
        for i in list(range(k + 1, blocks)) + list(range(k)):
            new = rows[i]
            for q in range(p):
                new = new - lanes(rows[i], p * k + q) * piv[q : q + 1, :]
            rows[i] = new
        rows[k] = piv
    return jnp.concatenate(rows, axis=0)


def update_kernel(
    members, bins, hx_ref, gathered_ref, spread_ref, resp_ref, obs_ref, weight_ref, x_ref,
    field_ref, finals_ref, left, anom, out, sems,
):
    sensors = weight_ref.shape[1]
    turn(gathered_ref, left)
    step = 512
    for c in range(0, sensors, step):
        cut = slice(c, c + step)
        hx = hx_ref[:, cut] + observe(members, bins, left, spread_ref, resp_ref, cut)
        center = sublane_mean(hx)
        anom[0:members, cut] = hx - center
        anom[members:, cut] = jnp.broadcast_to(center, (anom.shape[0] - members, step))
    cut = slice(sensors, sensors + 128)
    picked = hx_ref[:, cut] + observe(members, bins, left, spread_ref, resp_ref, cut)
    rhi, rlo = split(anom[...])
    whi, wlo = split(
        jnp.concatenate([anom[0:members, :] * weight_ref[t : t + 1, :] for t in range(2)], axis=0)
    )
    sums = (
        lax.dot_general(whi, rhi, NT, preferred_element_type=F32)
        + lax.dot_general(wlo, rhi, NT, preferred_element_type=F32)
        + lax.dot_general(whi, rlo, NT, preferred_element_type=F32)
    )
    pulls = (
        jnp.dot(whi, obs_ref[0], preferred_element_type=F32)
        + jnp.dot(wlo, obs_ref[0], preferred_element_type=F32)
        + jnp.dot(whi, obs_ref[1], preferred_element_type=F32)
    )
    lane = lax.broadcasted_iota(jnp.int32, (2 * members, 2 * members), 1)
    wide_sums = jnp.concatenate(
        [sums, jnp.zeros((2 * members, 2 * members - sums.shape[1]), F32)], axis=1
    )
    base = jnp.where(lane < members, wide_sums, pulls - sums[:, members : members + 1])
    lane = lane[0:members]
    right = lane >= members
    row = lax.broadcasted_iota(jnp.int32, lane.shape, 0)
    prior = jnp.where((lane == row) | (lane == row + members), members - 1.0, 0.0)
    even = jnp.where(right, 1.0 / members, 0.0)

    def mixer_t(solved):
        held = jnp.where(right, solved, 0.0)
        return held - sublane_mean(held) + even

    first_t = mixer_t(solve(base[0:members] + prior))
    tilt = jnp.sum(first_t, axis=1, keepdims=True) * (1.0 / members)
    first = first_t.T[members:, :]
    first_c = first - sublane_mean(first)
    moved = mm(first_c, base[members:])
    swapped = pltpu.roll(first_t, members, axis=1) - tilt
    crossed = mm(moved[:, 0:members], jnp.where(right, tilt, swapped))
    second_t = mixer_t(
        solve(prior + jnp.where(right, moved - crossed, crossed))
    )
    total = mm(second_t.T[members:, :], jnp.concatenate([first, first], axis=1))
    thi, tlo = split(total)
    lhs = jnp.concatenate([thi, tlo[:, 0:members]], axis=1)
    copies = []
    for first_bin in range(0, bins, bins // 2):
        group = range(first_bin, first_bin + bins // 2)
        for b in group:
            out[b] = jnp.dot(lhs, x_ref[b], preferred_element_type=F32)
        for b in group:
            copies.append(pltpu.make_async_copy(out.at[b], field_ref.at[:, b, :], sems.at[b]))
            copies[-1].start()
    finals_ref[...] = mm(total[:, 0:members], picked).T[0 : finals_ref.shape[0], :]
    for copy in copies:
        copy.wait()


def shards(state, kernel, blocks, foot_weight, bin_response, observed, obs_var, batch_order):
    members, bins, cells = state.shape
    nb = cells // BLK
    sensors = obs_var.shape[0]
    batches = sensors // P_SIZE
    nz, nc = lax.axis_size("zrow"), lax.axis_size("zcol")
    devices = nz * nc
    me = lax.axis_index(AXES)
    share = P_SIZE // devices
    zbits = [(nc << i).bit_length() - 1 for i in range(nz.bit_length() - 1)]
    cbits = [i for i in reversed(range(nc.bit_length() - 1))]
    rounds = [[bit] for bit in reversed(zbits)]
    plane = [bit for bit in cbits if bit > 0]
    while plane:
        rounds.append(sorted(plane[-2:]))
        plane = plane[:-2]
    bits = [bit for group in rounds for bit in group] + [0]
    rows = members * bins
    half = nb * devices // 2
    wide = 6 * half * sensors
    width = sensors + 128
    small = pltpu.CompilerParams(vmem_limit_bytes=8 * MIB + wide)
    large = pltpu.CompilerParams(vmem_limit_bytes=12 * MIB + 2 * wide)

    def cost(us):
        return pl.CostEstimate(flops=0, bytes_accessed=int(us * 3000000), transcendentals=0)

    def spread_of(first, who, places, weights):
        return pl.pallas_call(
            functools.partial(spread_kernel, bits, nb, first),
            out_shape=jax.ShapeDtypeStruct((3 * half, width), BF16),
            in_specs=[SMEM_SPEC, VMEM_SPEC, VMEM_SPEC],
            out_specs=VMEM_SPEC,
            compiler_params=small,
            name="spread",
            cost_estimate=cost(1.0),
        )(who, places, weights)

    def exchange(value, mask):
        return lax.ppermute(value, AXES, [(i, i ^ mask) for i in range(devices)])

    far_state = pltpu.with_memory_space_constraint(state, pltpu.HBM)
    staging = [pltpu.VMEM((bins, members, cells), F32), pltpu.SemaphoreType.DMA((bins,))]
    piece = pl.pallas_call(
        means_kernel,
        out_shape=jax.ShapeDtypeStruct((nb, rows), F32),
        in_specs=[HBM_SPEC, HBM_SPEC],
        out_specs=VMEM_SPEC,
        scratch_shapes=staging + [pltpu.VMEM((1, cells), F32), pltpu.SemaphoreType.DMA],
        compiler_params=small,
        name="means",
    )(far_state, pltpu.with_memory_space_constraint(kernel.reshape(1, cells), pltpu.HBM))

    who, places, weights = me.reshape(1), blocks.T, foot_weight.T
    orders = batch_order.reshape(sensors // 128, 128)
    inverse = obs_var.reshape(sensors // 128, 128)

    def roles_of(*args):
        return pl.pallas_call(
            functools.partial(roles_kernel, share),
            out_shape=[
                jax.ShapeDtypeStruct((batches, sensors), F32),
                jax.ShapeDtypeStruct((blocks.shape[1], width), jnp.int32),
                jax.ShapeDtypeStruct((blocks.shape[1], width), F32),
                jax.ShapeDtypeStruct((bins, width), F32),
            ],
            in_specs=[SMEM_SPEC] + [VMEM_SPEC] * 5,
            out_specs=[VMEM_SPEC] * 4,
            compiler_params=small,
            name="roles",
            cost_estimate=cost(0.6),
        )(*args)

    def obs_of(observed):
        return pl.pallas_call(
            obs_kernel,
            out_shape=jax.ShapeDtypeStruct((2, sensors, 2 * members), BF16),
            in_specs=[VMEM_SPEC],
            out_specs=VMEM_SPEC,
            compiler_params=small,
            name="observed",
            cost_estimate=cost(0.4),
        )(observed)

    def halves_of(far_state):
        return pl.pallas_call(
            halves_kernel,
            out_shape=jax.ShapeDtypeStruct((bins, 3 * members, cells), BF16),
            in_specs=[HBM_SPEC],
            out_specs=VMEM_SPEC,
            scratch_shapes=staging,
            compiler_params=small,
            name="halves",
            cost_estimate=cost(1.5),
        )(pltpu.with_memory_space_constraint(far_state, pltpu.HBM))

    made = {}

    def first_work():
        made["roles"] = roles_of(who, orders, inverse, places, weights, bin_response.T)
        made["near"] = spread_of(0, who, *made["roles"][1:3])

    def second_work():
        made["far"] = spread_of(half, who, *made["roles"][1:3])

    def third_work():
        made["parts"] = halves_of(state)
        made["obs"] = obs_of(observed.T)

    beside = [first_work, second_work, third_work]
    for i, group in enumerate(rounds):
        masks = [1 << bit for bit in group]
        if len(masks) == 2:
            masks.append(masks[0] | masks[1])
        if i == 0:
            piece, orders, places, weights = lax.optimization_barrier(
                (piece, orders, places, weights)
            )
        elif i == 1:
            piece, who = lax.optimization_barrier((piece, who))
        elif i == 2:
            piece, state, observed = lax.optimization_barrier((piece, state, observed))
        others = [exchange(piece, mask) for mask in masks]
        if i < len(beside):
            beside[i]()
        others, made = lax.optimization_barrier((others, made))
        piece = jnp.concatenate([piece] + others, axis=0)
    weight, _, _, resp = made["roles"]
    other = exchange(piece, 1)

    left = pltpu.VMEM((rows, 3 * half), BF16)
    hx = pl.pallas_call(
        functools.partial(partial_kernel, members, bins),
        out_shape=jax.ShapeDtypeStruct((members, width), F32),
        in_specs=[VMEM_SPEC] * 3,
        out_specs=VMEM_SPEC,
        scratch_shapes=[left],
        compiler_params=large,
        name="partial",
        cost_estimate=cost(1.2),
    )(piece, made["near"], resp)

    field, finals = pl.pallas_call(
        functools.partial(update_kernel, members, bins),
        out_shape=[
            jax.ShapeDtypeStruct((members, bins, cells), F32),
            jax.ShapeDtypeStruct((batches * share, members), F32),
        ],
        in_specs=[VMEM_SPEC] * 7,
        out_specs=[HBM_SPEC, VMEM_SPEC],
        scratch_shapes=[
            left,
            pltpu.VMEM((members + 16, sensors), F32),
            pltpu.VMEM((bins, members, cells), F32),
            pltpu.SemaphoreType.DMA((bins,)),
        ],
        compiler_params=large,
        name="update",
    )(hx, other, made["far"], resp, made["obs"], weight, made["parts"])
    return (field, finals.reshape(batches, share, members).transpose(0, 2, 1))


def solution(mesh):
    return jax.shard_map(
        shards,
        mesh=mesh,
        in_specs=(
            P(None, None, AXES),
            P(AXES),
            P(),
            P(),
            P(),
            P(),
            P(),
            P(),
        ),
        out_specs=(P(None, None, AXES), P(None, None, AXES)),
        check_vma=False,
    )
```

```python
import functools

import jax
import jax.numpy as jnp
from jax import lax
from jax.experimental import pallas as pl
from jax.experimental.pallas import tpu as pltpu
from jax.sharding import PartitionSpec as P

BLK = 128
P_SIZE = 1024
AXES = ("zrow", "zcol")
F32 = jnp.float32
BF16 = jnp.bfloat16
NT = (((1,), (1,)), ((), ()))
VMEM_SPEC = pl.BlockSpec(memory_space=pltpu.VMEM)
HBM_SPEC = pl.BlockSpec(memory_space=pltpu.HBM)
SMEM_SPEC = pl.BlockSpec(memory_space=pltpu.SMEM)
MIB = 1024 * 1024


def split(x):
    hi = x.astype(BF16)
    return hi, (x - hi.astype(F32)).astype(BF16)


def mm(a, b):
    return jnp.dot(a, b, precision=lax.Precision.HIGHEST, preferred_element_type=F32)


def sublane_mean(x):
    return jnp.sum(x, axis=0, keepdims=True) * (1.0 / x.shape[0])


def lane_mean(x):
    return jnp.sum(x, axis=1, keepdims=True) * (1.0 / x.shape[1])


def means_kernel(x_ref, kernel_ref, out_ref, held_ref, sems, weight_ref, sem):
    members, bins, _ = x_ref.shape
    nb = out_ref.shape[0]
    kernel_copy = pltpu.make_async_copy(kernel_ref, weight_ref, sem)
    kernel_copy.start()
    copies = []
    for b in range(bins):
        copies.append(pltpu.make_async_copy(x_ref.at[:, b, :], held_ref.at[b], sems.at[b]))
        copies[-1].start()
    kernel_copy.wait()
    scale = weight_ref[...] * (1.0 / BLK)
    lane = lax.broadcasted_iota(jnp.int32, (2 * members, 128), 1)
    for b in range(0, bins, 2):
        copies[b].wait()
        copies[b + 1].wait()
        total = jnp.zeros((2 * members, 128), F32)
        for j in range(nb):
            cut = slice(j * BLK, (j + 1) * BLK)
            x = jnp.concatenate([held_ref[b, :, cut], held_ref[b + 1, :, cut]], axis=0)
            summed = jnp.sum(x * scale[:, cut], axis=1, keepdims=True)
            total = jnp.where(lane == j, summed, total)
        out_ref[:, b * members : (b + 2) * members] = total.T[0:nb, :]


def spread_kernel(bits, nb, first, me_ref, blocks_ref, weight_ref, out_ref):
    foot, sensors = blocks_ref.shape
    half = out_ref.shape[0] // 3
    step = 128
    for c in range(0, sensors, step):
        blk = blocks_ref[:, c : c + step]
        away = lax.shift_right_logical(blk, nb.bit_length() - 1) ^ me_ref[0]
        place = blk & (nb - 1)
        for i, bit in enumerate(bits):
            place += (lax.shift_right_logical(away, bit) & 1) * (nb << i)
        weight = weight_ref[:, c : c + step]
        for r in range(0, half, 128):
            row = lax.broadcasted_iota(jnp.int32, (128, step), 0) + (r + first)
            total = jnp.where(row == place[0:1, :], weight[0:1, :], 0.0)
            for f in range(1, foot):
                total += jnp.where(row == place[f : f + 1, :], weight[f : f + 1, :], 0.0)
            hi, low = split(total)
            out_ref[r : r + 128, c : c + step] = hi
            out_ref[half + r : half + r + 128, c : c + step] = low
            out_ref[2 * half + r : 2 * half + r + 128, c : c + step] = hi


def halves_kernel(x_ref, out_ref, held_ref, sems):
    members, bins, _ = x_ref.shape
    copies = []
    for b in range(bins):
        copies.append(pltpu.make_async_copy(x_ref.at[:, b, :], held_ref.at[b], sems.at[b]))
        copies[-1].start()
    for b in range(bins):
        copies[b].wait()
        hi, low = split(held_ref[b])
        out_ref[b, 0:members, :] = hi
        out_ref[b, members : 2 * members, :] = low
        out_ref[b, 2 * members : 3 * members, :] = hi


def roles_kernel(share, me_ref, orders_ref, var_ref, blocks_ref, foot_ref, resp_ref, weight_ref, *table_refs):
    batches = weight_ref.shape[0]
    groups = var_ref.shape[0]
    each = groups // batches
    per = each * 128
    sensors = blocks_ref.shape[1]
    start = me_ref[0] * share
    lane = lax.broadcasted_iota(jnp.int32, (8, 128), 1)
    own = jnp.full((8, 128), -1, jnp.int32)
    inverse = 1.0 / var_ref[...]
    high = lax.broadcasted_iota(jnp.int32, (groups, per), 0)
    low = lax.broadcasted_iota(jnp.int32, (128, per), 0)
    for t in range(batches):
        order = jnp.concatenate(
            [orders_ref[g : g + 1, :] for g in range(t * each, (t + 1) * each)], axis=1
        )
        mine = orders_ref[pl.ds(t * each + lax.shift_right_logical(start, 7), 1), :]
        mine = pltpu.roll(
            jnp.broadcast_to(mine, (8, 128)), (t * share - (start & 127)) & 127, axis=1
        )
        own = jnp.where((lane >= t * share) & (lane < (t + 1) * share), mine, own)
        of_high = jnp.where(high == lax.shift_right_logical(order, 7), 1.0, 0.0).astype(BF16)
        of_low = jnp.where(low == (order & 127), 1.0, 0.0).astype(BF16)
        held = lax.dot_general(of_high, of_low, NT, preferred_element_type=F32) * inverse
        for g in range(groups):
            weight_ref[t : t + 1, g * 128 : (g + 1) * 128] = held[g : g + 1, :]
    sensor = lax.broadcasted_iota(jnp.int32, (sensors, 128), 0)
    pick = jnp.where(sensor == own[0:1, :], 1.0, 0.0).astype(BF16)
    tables = jnp.concatenate(
        [blocks_ref[...].astype(F32), foot_ref[...], resp_ref[...]], axis=0
    )
    first = tables.astype(BF16)
    rest = tables - first.astype(F32)
    second = rest.astype(BF16)
    third = (rest - second.astype(F32)).astype(BF16)
    stacked = jnp.dot(
        jnp.concatenate([first, second, third], axis=0), pick, preferred_element_type=F32
    )
    n = tables.shape[0]
    chosen = stacked[0:n] + stacked[n : 2 * n] + stacked[2 * n : 3 * n]
    at = 0
    for ref, table in zip(table_refs, (blocks_ref, foot_ref, resp_ref)):
        rows = table.shape[0]
        ref[:, 0:sensors] = table[...]
        ref[:, sensors : sensors + 128] = chosen[at : at + rows].astype(ref.dtype)
        at += rows


def obs_kernel(obs_ref, out_ref):
    members = obs_ref.shape[0]
    step = 128
    for c in range(0, obs_ref.shape[1], step):
        turned = obs_ref[:, c : c + step].T
        hi, low = split(jnp.concatenate([jnp.zeros_like(turned), turned], axis=1))
        out_ref[0, c : c + step, :] = hi
        out_ref[1, c : c + step, :] = low


def turn(gathered_ref, left):
    half = gathered_ref.shape[0]
    for r in range(0, half, 128):
        hi, low = split(gathered_ref[r : r + 128, :].T)
        left[:, r : r + 128] = hi
        left[:, half + r : half + r + 128] = hi
        left[:, 2 * half + r : 2 * half + r + 128] = low


def observe(members, bins, left, spread_ref, resp_ref, cut):
    z = jnp.dot(left[...], spread_ref[:, cut], preferred_element_type=F32)
    hx = z[0:members, :] * resp_ref[0:1, cut]
    for b in range(1, bins):
        hx += z[b * members : (b + 1) * members, :] * resp_ref[b : b + 1, cut]
    return hx


def partial_kernel(members, bins, gathered_ref, spread_ref, resp_ref, hx_ref, left):
    turn(gathered_ref, left)
    width = resp_ref.shape[1]
    for c in range(0, width, 512):
        cut = slice(c, min(c + 512, width))
        hx_ref[:, cut] = observe(members, bins, left, spread_ref, resp_ref, cut)


def solve(aug):
    n, width = aug.shape
    p = 16
    blocks = n // p
    rows = [aug[p * i : p * i + p, :] for i in range(blocks)]
    sub = lax.broadcasted_iota(jnp.int32, (p, width), 0)

    def lanes(x, j):
        return jnp.broadcast_to(x[:, j : j + 1], (p, width))

    for k in range(blocks):
        piv = rows[k]
        own = [lanes(piv, p * k + q) for q in range(p)]
        for q in range(p):
            here = sub == q
            mult = own[q]
            inv = 1.0 / mult[q : q + 1, :]
            scaled = piv[q : q + 1, :] * inv
            piv = jnp.where(here, scaled, piv - mult * scaled)
            for r in range(q + 1, p):
                scaled = own[r][q : q + 1, :] * inv
                own[r] = jnp.where(here, scaled, own[r] - mult * scaled)
        for i in list(range(k + 1, blocks)) + list(range(k)):
            new = rows[i]
            for q in range(p):
                new = new - lanes(rows[i], p * k + q) * piv[q : q + 1, :]
            rows[i] = new
        rows[k] = piv
    return jnp.concatenate(rows, axis=0)


def update_kernel(
    members, bins, hx_ref, gathered_ref, spread_ref, resp_ref, obs_ref, weight_ref, x_ref,
    field_ref, finals_ref, left, anom, out, own, sems,
):
    sensors = weight_ref.shape[1]
    turn(gathered_ref, left)
    step = 512
    for c in range(0, sensors, step):
        cut = slice(c, c + step)
        hx = hx_ref[:, cut] + observe(members, bins, left, spread_ref, resp_ref, cut)
        center = sublane_mean(hx)
        anom[0:members, cut] = hx - center
        anom[members:, cut] = jnp.broadcast_to(center, (anom.shape[0] - members, step))
    rhi, rlo = split(anom[...])
    whi, wlo = split(
        jnp.concatenate([anom[0:members, :] * weight_ref[t : t + 1, :] for t in range(2)], axis=0)
    )
    sums = (
        lax.dot_general(whi, rhi, NT, preferred_element_type=F32)
        + lax.dot_general(wlo, rhi, NT, preferred_element_type=F32)
        + lax.dot_general(whi, rlo, NT, preferred_element_type=F32)
    )
    pulls = (
        jnp.dot(whi, obs_ref[0], preferred_element_type=F32)
        + jnp.dot(wlo, obs_ref[0], preferred_element_type=F32)
        + jnp.dot(whi, obs_ref[1], preferred_element_type=F32)
    )
    lane = lax.broadcasted_iota(jnp.int32, (2 * members, 2 * members), 1)
    wide_sums = jnp.concatenate(
        [sums, jnp.zeros((2 * members, 2 * members - sums.shape[1]), F32)], axis=1
    )
    base = jnp.where(lane < members, wide_sums, pulls - sums[:, members : members + 1])
    lane = lane[0:members]
    right = lane >= members
    row = lax.broadcasted_iota(jnp.int32, lane.shape, 0)
    prior = jnp.where((lane == row) | (lane == row + members), members - 1.0, 0.0)
    even = jnp.where(right, 1.0 / members, 0.0)

    def mixer_t(solved):
        held = jnp.where(right, solved, 0.0)
        return held - sublane_mean(held) + even

    first_t = mixer_t(solve(base[0:members] + prior))
    tilt = jnp.sum(first_t, axis=1, keepdims=True) * (1.0 / members)
    first = first_t.T[members:, :]
    first_c = first - sublane_mean(first)
    moved = mm(first_c, base[members:])
    swapped = pltpu.roll(first_t, members, axis=1) - tilt
    crossed = mm(moved[:, 0:members], jnp.where(right, tilt, swapped))
    second_t = mixer_t(
        solve(prior + jnp.where(right, moved - crossed, crossed))
    )
    total = mm(second_t.T[members:, :], jnp.concatenate([first, first], axis=1))
    thi, tlo = split(total)
    lhs = jnp.concatenate([thi, tlo[:, 0:members]], axis=1)
    copies = []
    for first_bin in range(0, bins, bins // 2):
        group = range(first_bin, first_bin + bins // 2)
        for b in group:
            out[b] = jnp.dot(lhs, x_ref[b], preferred_element_type=F32)
        for b in group:
            copies.append(pltpu.make_async_copy(out.at[b], field_ref.at[:, b, :], sems.at[b]))
            copies[-1].start()
    cut = slice(sensors, sensors + 128)
    picked = hx_ref[:, cut] + observe(members, bins, left, spread_ref, resp_ref, cut)
    own[...] = mm(total[:, 0:members], picked).T[0 : own.shape[0], :]
    copies.append(pltpu.make_async_copy(own, finals_ref, sems.at[bins]))
    copies[-1].start()
    for copy in copies:
        copy.wait()


def shards(state, kernel, blocks, foot_weight, bin_response, observed, obs_var, batch_order):
    members, bins, cells = state.shape
    nb = cells // BLK
    sensors = obs_var.shape[0]
    batches = sensors // P_SIZE
    nz, nc = lax.axis_size("zrow"), lax.axis_size("zcol")
    devices = nz * nc
    me = lax.axis_index(AXES)
    share = P_SIZE // devices
    zbits = [(nc << i).bit_length() - 1 for i in range(nz.bit_length() - 1)]
    cbits = [i for i in reversed(range(nc.bit_length() - 1))]
    rounds = [[bit] for bit in reversed(zbits)]
    plane = [bit for bit in cbits if bit > 0]
    while plane:
        rounds.append(sorted(plane[-2:]))
        plane = plane[:-2]
    bits = [bit for group in rounds for bit in group] + [0]
    rows = members * bins
    half = nb * devices // 2
    wide = 6 * half * sensors
    width = sensors + 128
    small = pltpu.CompilerParams(vmem_limit_bytes=8 * MIB + wide)
    large = pltpu.CompilerParams(vmem_limit_bytes=12 * MIB + 2 * wide)

    def cost(us):
        return pl.CostEstimate(flops=0, bytes_accessed=int(us * 3000000), transcendentals=0)

    def spread_of(first, who, places, weights):
        return pl.pallas_call(
            functools.partial(spread_kernel, bits, nb, first),
            out_shape=jax.ShapeDtypeStruct((3 * half, width), BF16),
            in_specs=[SMEM_SPEC, VMEM_SPEC, VMEM_SPEC],
            out_specs=VMEM_SPEC,
            compiler_params=small,
            name="spread",
            cost_estimate=cost(1.0),
        )(who, places, weights)

    def exchange(value, mask):
        return lax.ppermute(value, AXES, [(i, i ^ mask) for i in range(devices)])

    far_state = pltpu.with_memory_space_constraint(state, pltpu.HBM)
    staging = [pltpu.VMEM((bins, members, cells), F32), pltpu.SemaphoreType.DMA((bins,))]
    piece = pl.pallas_call(
        means_kernel,
        out_shape=jax.ShapeDtypeStruct((nb, rows), F32),
        in_specs=[HBM_SPEC, HBM_SPEC],
        out_specs=VMEM_SPEC,
        scratch_shapes=staging + [pltpu.VMEM((1, cells), F32), pltpu.SemaphoreType.DMA],
        compiler_params=small,
        name="means",
    )(far_state, pltpu.with_memory_space_constraint(kernel.reshape(1, cells), pltpu.HBM))

    who, places, weights = me.reshape(1), blocks.T, foot_weight.T
    orders = batch_order.reshape(sensors // 128, 128)
    inverse = obs_var.reshape(sensors // 128, 128)

    def roles_of(*args):
        return pl.pallas_call(
            functools.partial(roles_kernel, share),
            out_shape=[
                jax.ShapeDtypeStruct((batches, sensors), F32),
                jax.ShapeDtypeStruct((blocks.shape[1], width), jnp.int32),
                jax.ShapeDtypeStruct((blocks.shape[1], width), F32),
                jax.ShapeDtypeStruct((bins, width), F32),
            ],
            in_specs=[SMEM_SPEC] + [VMEM_SPEC] * 5,
            out_specs=[VMEM_SPEC] * 4,
            compiler_params=small,
            name="roles",
            cost_estimate=cost(0.6),
        )(*args)

    def obs_of(observed):
        return pl.pallas_call(
            obs_kernel,
            out_shape=jax.ShapeDtypeStruct((2, sensors, 2 * members), BF16),
            in_specs=[VMEM_SPEC],
            out_specs=VMEM_SPEC,
            compiler_params=small,
            name="observed",
            cost_estimate=cost(0.4),
        )(observed)

    def halves_of(far_state):
        return pl.pallas_call(
            halves_kernel,
            out_shape=jax.ShapeDtypeStruct((bins, 3 * members, cells), BF16),
            in_specs=[HBM_SPEC],
            out_specs=VMEM_SPEC,
            scratch_shapes=staging,
            compiler_params=small,
            name="halves",
            cost_estimate=cost(1.5),
        )(pltpu.with_memory_space_constraint(far_state, pltpu.HBM))

    made = {}

    def first_work():
        made["roles"] = roles_of(who, orders, inverse, places, weights, bin_response.T)
        made["near"] = spread_of(0, who, *made["roles"][1:3])

    def second_work():
        made["far"] = spread_of(half, who, *made["roles"][1:3])

    def third_work():
        made["parts"] = halves_of(state)
        made["obs"] = obs_of(observed.T)

    beside = [first_work, second_work, third_work]
    for i, group in enumerate(rounds):
        masks = [1 << bit for bit in group]
        if len(masks) == 2:
            masks.append(masks[0] | masks[1])
        if i == 0:
            piece, orders, places, weights = lax.optimization_barrier(
                (piece, orders, places, weights)
            )
        elif i == 1:
            piece, who = lax.optimization_barrier((piece, who))
        elif i == 2:
            piece, state, observed = lax.optimization_barrier((piece, state, observed))
        others = [exchange(piece, mask) for mask in masks]
        if i < len(beside):
            beside[i]()
        others, made = lax.optimization_barrier((others, made))
        piece = jnp.concatenate([piece] + others, axis=0)
    weight, _, _, resp = made["roles"]
    other = exchange(piece, 1)

    left = pltpu.VMEM((rows, 3 * half), BF16)
    hx = pl.pallas_call(
        functools.partial(partial_kernel, members, bins),
        out_shape=jax.ShapeDtypeStruct((members, width), F32),
        in_specs=[VMEM_SPEC] * 3,
        out_specs=VMEM_SPEC,
        scratch_shapes=[left],
        compiler_params=large,
        name="partial",
        cost_estimate=cost(1.2),
    )(piece, made["near"], resp)

    field, finals = pl.pallas_call(
        functools.partial(update_kernel, members, bins),
        out_shape=[
            jax.ShapeDtypeStruct((members, bins, cells), F32),
            jax.ShapeDtypeStruct((batches * share, members), F32),
        ],
        in_specs=[VMEM_SPEC] * 7,
        out_specs=[HBM_SPEC, HBM_SPEC],
        scratch_shapes=[
            left,
            pltpu.VMEM((members + 16, sensors), F32),
            pltpu.VMEM((bins, members, cells), F32),
            pltpu.VMEM((batches * share, members), F32),
            pltpu.SemaphoreType.DMA((bins + 1,)),
        ],
        compiler_params=large,
        name="update",
    )(hx, other, made["far"], resp, made["obs"], weight, made["parts"])
    return (field, finals.reshape(batches, share, members).transpose(0, 2, 1))


def solution(mesh):
    return jax.shard_map(
        shards,
        mesh=mesh,
        in_specs=(
            P(None, None, AXES),
            P(AXES),
            P(),
            P(),
            P(),
            P(),
            P(),
            P(),
        ),
        out_specs=(P(None, None, AXES), P(None, None, AXES)),
        check_vma=False,
    )
```

```python
import functools

import jax
import jax.numpy as jnp
from jax import lax
from jax.experimental import pallas as pl
from jax.experimental.pallas import tpu as pltpu
from jax.sharding import PartitionSpec as P

BLK = 128
P_SIZE = 1024
AXES = ("zrow", "zcol")
F32 = jnp.float32
BF16 = jnp.bfloat16
NT = (((1,), (1,)), ((), ()))
VMEM_SPEC = pl.BlockSpec(memory_space=pltpu.VMEM)
HBM_SPEC = pl.BlockSpec(memory_space=pltpu.HBM)
SMEM_SPEC = pl.BlockSpec(memory_space=pltpu.SMEM)
MIB = 1024 * 1024


def split(x):
    hi = x.astype(BF16)
    return hi, (x - hi.astype(F32)).astype(BF16)


def mm(a, b):
    ahi, alo = split(a)
    bhi, blo = split(b)
    return (
        jnp.dot(ahi, bhi, preferred_element_type=F32)
        + jnp.dot(ahi, blo, preferred_element_type=F32)
        + jnp.dot(alo, bhi, preferred_element_type=F32)
    )


def sublane_mean(x):
    return jnp.sum(x, axis=0, keepdims=True) * (1.0 / x.shape[0])


def lane_mean(x):
    return jnp.sum(x, axis=1, keepdims=True) * (1.0 / x.shape[1])


def means_kernel(x_ref, kernel_ref, out_ref, held_ref, sems, weight_ref, sem):
    members, bins, _ = x_ref.shape
    nb = out_ref.shape[0]
    kernel_copy = pltpu.make_async_copy(kernel_ref, weight_ref, sem)
    kernel_copy.start()
    copies = []
    for b in range(bins):
        copies.append(pltpu.make_async_copy(x_ref.at[:, b, :], held_ref.at[b], sems.at[b]))
        copies[-1].start()
    kernel_copy.wait()
    scale = weight_ref[...] * (1.0 / BLK)
    lane = lax.broadcasted_iota(jnp.int32, (2 * members, 128), 1)
    for b in range(0, bins, 2):
        copies[b].wait()
        copies[b + 1].wait()
        total = jnp.zeros((2 * members, 128), F32)
        for j in range(nb):
            cut = slice(j * BLK, (j + 1) * BLK)
            x = jnp.concatenate([held_ref[b, :, cut], held_ref[b + 1, :, cut]], axis=0)
            summed = jnp.sum(x * scale[:, cut], axis=1, keepdims=True)
            total = jnp.where(lane == j, summed, total)
        out_ref[:, b * members : (b + 2) * members] = total.T[0:nb, :]


def spread_kernel(bits, nb, first, me_ref, blocks_ref, weight_ref, out_ref):
    foot, sensors = blocks_ref.shape
    half = out_ref.shape[0] // 3
    step = 128
    for c in range(0, sensors, step):
        blk = blocks_ref[:, c : c + step]
        away = lax.shift_right_logical(blk, nb.bit_length() - 1) ^ me_ref[0]
        place = blk & (nb - 1)
        for i, bit in enumerate(bits):
            place += (lax.shift_right_logical(away, bit) & 1) * (nb << i)
        weight = weight_ref[:, c : c + step]
        for r in range(0, half, 128):
            row = lax.broadcasted_iota(jnp.int32, (128, step), 0) + (r + first)
            total = jnp.where(row == place[0:1, :], weight[0:1, :], 0.0)
            for f in range(1, foot):
                total += jnp.where(row == place[f : f + 1, :], weight[f : f + 1, :], 0.0)
            hi, low = split(total)
            out_ref[r : r + 128, c : c + step] = hi
            out_ref[half + r : half + r + 128, c : c + step] = low
            out_ref[2 * half + r : 2 * half + r + 128, c : c + step] = hi


def halves_kernel(x_ref, out_ref, held_ref, sems):
    members, bins, _ = x_ref.shape
    copies = []
    for b in range(bins):
        copies.append(pltpu.make_async_copy(x_ref.at[:, b, :], held_ref.at[b], sems.at[b]))
        copies[-1].start()
    for b in range(bins):
        copies[b].wait()
        hi, low = split(held_ref[b])
        out_ref[b, 0:members, :] = hi
        out_ref[b, members : 2 * members, :] = low
        out_ref[b, 2 * members : 3 * members, :] = hi


def roles_kernel(share, me_ref, orders_ref, var_ref, blocks_ref, foot_ref, resp_ref, weight_ref, *table_refs):
    batches = weight_ref.shape[0]
    groups = var_ref.shape[0]
    each = groups // batches
    per = each * 128
    sensors = blocks_ref.shape[1]
    start = me_ref[0] * share
    lane = lax.broadcasted_iota(jnp.int32, (8, 128), 1)
    own = jnp.full((8, 128), -1, jnp.int32)
    inverse = 1.0 / var_ref[...]
    high = lax.broadcasted_iota(jnp.int32, (groups, per), 0)
    low = lax.broadcasted_iota(jnp.int32, (128, per), 0)
    for t in range(batches):
        order = jnp.concatenate(
            [orders_ref[g : g + 1, :] for g in range(t * each, (t + 1) * each)], axis=1
        )
        mine = orders_ref[pl.ds(t * each + lax.shift_right_logical(start, 7), 1), :]
        mine = pltpu.roll(
            jnp.broadcast_to(mine, (8, 128)), (t * share - (start & 127)) & 127, axis=1
        )
        own = jnp.where((lane >= t * share) & (lane < (t + 1) * share), mine, own)
        of_high = jnp.where(high == lax.shift_right_logical(order, 7), 1.0, 0.0).astype(BF16)
        of_low = jnp.where(low == (order & 127), 1.0, 0.0).astype(BF16)
        held = lax.dot_general(of_high, of_low, NT, preferred_element_type=F32) * inverse
        for g in range(groups):
            weight_ref[t : t + 1, g * 128 : (g + 1) * 128] = held[g : g + 1, :]
    sensor = lax.broadcasted_iota(jnp.int32, (sensors, 128), 0)
    pick = jnp.where(sensor == own[0:1, :], 1.0, 0.0).astype(BF16)
    tables = jnp.concatenate(
        [blocks_ref[...].astype(F32), foot_ref[...], resp_ref[...]], axis=0
    )
    first = tables.astype(BF16)
    rest = tables - first.astype(F32)
    second = rest.astype(BF16)
    third = (rest - second.astype(F32)).astype(BF16)
    stacked = jnp.dot(
        jnp.concatenate([first, second, third], axis=0), pick, preferred_element_type=F32
    )
    n = tables.shape[0]
    chosen = stacked[0:n] + stacked[n : 2 * n] + stacked[2 * n : 3 * n]
    at = 0
    for ref, table in zip(table_refs, (blocks_ref, foot_ref, resp_ref)):
        rows = table.shape[0]
        ref[:, 0:sensors] = table[...]
        ref[:, sensors : sensors + 128] = chosen[at : at + rows].astype(ref.dtype)
        at += rows


def obs_kernel(obs_ref, out_ref):
    members = obs_ref.shape[0]
    step = 128
    for c in range(0, obs_ref.shape[1], step):
        turned = obs_ref[:, c : c + step].T
        hi, low = split(jnp.concatenate([jnp.zeros_like(turned), turned], axis=1))
        out_ref[0, c : c + step, :] = hi
        out_ref[1, c : c + step, :] = low


def turn(gathered_ref, left):
    half = gathered_ref.shape[0]
    for r in range(0, half, 128):
        hi, low = split(gathered_ref[r : r + 128, :].T)
        left[:, r : r + 128] = hi
        left[:, half + r : half + r + 128] = hi
        left[:, 2 * half + r : 2 * half + r + 128] = low


def observe(members, bins, left, spread_ref, resp_ref, cut):
    z = jnp.dot(left[...], spread_ref[:, cut], preferred_element_type=F32)
    hx = z[0:members, :] * resp_ref[0:1, cut]
    for b in range(1, bins):
        hx += z[b * members : (b + 1) * members, :] * resp_ref[b : b + 1, cut]
    return hx


def partial_kernel(members, bins, gathered_ref, spread_ref, resp_ref, hx_ref, left):
    turn(gathered_ref, left)
    width = resp_ref.shape[1]
    for c in range(0, width, 512):
        cut = slice(c, min(c + 512, width))
        hx_ref[:, cut] = observe(members, bins, left, spread_ref, resp_ref, cut)


def solve(aug):
    n, width = aug.shape
    p = 16
    blocks = n // p
    rows = [aug[p * i : p * i + p, :] for i in range(blocks)]
    sub = lax.broadcasted_iota(jnp.int32, (p, width), 0)

    def lanes(x, j):
        return jnp.broadcast_to(x[:, j : j + 1], (p, width))

    for k in range(blocks):
        piv = rows[k]
        own = [lanes(piv, p * k + q) for q in range(p)]
        for q in range(p):
            here = sub == q
            mult = own[q]
            inv = 1.0 / mult[q : q + 1, :]
            scaled = piv[q : q + 1, :] * inv
            piv = jnp.where(here, scaled, piv - mult * scaled)
            for r in range(q + 1, p):
                scaled = own[r][q : q + 1, :] * inv
                own[r] = jnp.where(here, scaled, own[r] - mult * scaled)
        for i in list(range(k + 1, blocks)) + list(range(k)):
            new = rows[i]
            for q in range(p):
                new = new - lanes(rows[i], p * k + q) * piv[q : q + 1, :]
            rows[i] = new
        rows[k] = piv
    return jnp.concatenate(rows, axis=0)


def update_kernel(
    members, bins, hx_ref, gathered_ref, spread_ref, resp_ref, obs_ref, weight_ref, x_ref,
    field_ref, finals_ref, left, anom, out, own, sems,
):
    sensors = weight_ref.shape[1]
    turn(gathered_ref, left)
    step = 512
    for c in range(0, sensors, step):
        cut = slice(c, c + step)
        hx = hx_ref[:, cut] + observe(members, bins, left, spread_ref, resp_ref, cut)
        center = sublane_mean(hx)
        anom[0:members, cut] = hx - center
        anom[members:, cut] = jnp.broadcast_to(center, (members, step))
    rhi, rlo = split(anom[...])
    whi, wlo = split(
        jnp.concatenate([anom[0:members, :] * weight_ref[t : t + 1, :] for t in range(2)], axis=0)
    )
    sums = (
        lax.dot_general(whi, rhi, NT, preferred_element_type=F32)
        + lax.dot_general(wlo, rhi, NT, preferred_element_type=F32)
        + lax.dot_general(whi, rlo, NT, preferred_element_type=F32)
    )
    pulls = (
        jnp.dot(whi, obs_ref[0], preferred_element_type=F32)
        + jnp.dot(wlo, obs_ref[0], preferred_element_type=F32)
        + jnp.dot(whi, obs_ref[1], preferred_element_type=F32)
    )
    lane = lax.broadcasted_iota(jnp.int32, (2 * members, 2 * members), 1)
    base = jnp.where(lane < members, sums, pulls - sums)
    lane = lane[0:members]
    right = lane >= members
    row = lax.broadcasted_iota(jnp.int32, lane.shape, 0)
    prior = jnp.where((lane == row) | (lane == row + members), members - 1.0, 0.0)
    even = jnp.where(right, 1.0 / members, 0.0)

    def mixer_t(solved):
        held = jnp.where(right, solved, 0.0)
        return held - sublane_mean(held) + even

    first_t = mixer_t(solve(base[0:members] + prior))
    tilt = jnp.sum(first_t, axis=1, keepdims=True) * (1.0 / members)
    first = first_t.T[members:, :]
    first_c = first - sublane_mean(first)
    moved = mm(first_c, base[members:])
    swapped = pltpu.roll(first_t, members, axis=1) - tilt
    crossed = mm(moved[:, 0:members], jnp.where(right, tilt, swapped))
    second_t = mixer_t(
        solve(prior + jnp.where(right, moved - crossed, crossed))
    )
    total = mm(second_t.T[members:, :], jnp.concatenate([first, first], axis=1))
    thi, tlo = split(total)
    lhs = jnp.concatenate([thi, tlo[:, 0:members]], axis=1)
    copies = []
    for first_bin in range(0, bins, bins // 2):
        group = range(first_bin, first_bin + bins // 2)
        for b in group:
            out[b] = jnp.dot(lhs, x_ref[b], preferred_element_type=F32)
        for b in group:
            copies.append(pltpu.make_async_copy(out.at[b], field_ref.at[:, b, :], sems.at[b]))
            copies[-1].start()
    cut = slice(sensors, sensors + 128)
    picked = hx_ref[:, cut] + observe(members, bins, left, spread_ref, resp_ref, cut)
    own[...] = mm(total[:, 0:members], picked).T[0 : own.shape[0], :]
    copies.append(pltpu.make_async_copy(own, finals_ref, sems.at[bins]))
    copies[-1].start()
    for copy in copies:
        copy.wait()


def shards(state, kernel, blocks, foot_weight, bin_response, observed, obs_var, batch_order):
    members, bins, cells = state.shape
    nb = cells // BLK
    sensors = obs_var.shape[0]
    batches = sensors // P_SIZE
    nz, nc = lax.axis_size("zrow"), lax.axis_size("zcol")
    devices = nz * nc
    me = lax.axis_index(AXES)
    share = P_SIZE // devices
    zbits = [(nc << i).bit_length() - 1 for i in range(nz.bit_length() - 1)]
    cbits = [i for i in reversed(range(nc.bit_length() - 1))]
    rounds = [[bit] for bit in reversed(zbits)]
    plane = [bit for bit in cbits if bit > 0]
    while plane:
        rounds.append(sorted(plane[-2:]))
        plane = plane[:-2]
    bits = [bit for group in rounds for bit in group] + [0]
    rows = members * bins
    half = nb * devices // 2
    wide = 6 * half * sensors
    width = sensors + 128
    small = pltpu.CompilerParams(vmem_limit_bytes=8 * MIB + wide)
    large = pltpu.CompilerParams(vmem_limit_bytes=12 * MIB + 2 * wide)

    def cost(us):
        return pl.CostEstimate(flops=0, bytes_accessed=int(us * 3000000), transcendentals=0)

    def spread_of(first, who, places, weights):
        return pl.pallas_call(
            functools.partial(spread_kernel, bits, nb, first),
            out_shape=jax.ShapeDtypeStruct((3 * half, width), BF16),
            in_specs=[SMEM_SPEC, VMEM_SPEC, VMEM_SPEC],
            out_specs=VMEM_SPEC,
            compiler_params=small,
            name="spread",
            cost_estimate=cost(1.0),
        )(who, places, weights)

    def exchange(value, mask):
        return lax.ppermute(value, AXES, [(i, i ^ mask) for i in range(devices)])

    far_state = pltpu.with_memory_space_constraint(state, pltpu.HBM)
    staging = [pltpu.VMEM((bins, members, cells), F32), pltpu.SemaphoreType.DMA((bins,))]
    piece = pl.pallas_call(
        means_kernel,
        out_shape=jax.ShapeDtypeStruct((nb, rows), F32),
        in_specs=[HBM_SPEC, HBM_SPEC],
        out_specs=VMEM_SPEC,
        scratch_shapes=staging + [pltpu.VMEM((1, cells), F32), pltpu.SemaphoreType.DMA],
        compiler_params=small,
        name="means",
    )(far_state, pltpu.with_memory_space_constraint(kernel.reshape(1, cells), pltpu.HBM))

    who, places, weights = me.reshape(1), blocks.T, foot_weight.T
    orders = batch_order.reshape(sensors // 128, 128)
    inverse = obs_var.reshape(sensors // 128, 128)

    def roles_of(*args):
        return pl.pallas_call(
            functools.partial(roles_kernel, share),
            out_shape=[
                jax.ShapeDtypeStruct((batches, sensors), F32),
                jax.ShapeDtypeStruct((blocks.shape[1], width), jnp.int32),
                jax.ShapeDtypeStruct((blocks.shape[1], width), F32),
                jax.ShapeDtypeStruct((bins, width), F32),
            ],
            in_specs=[SMEM_SPEC] + [VMEM_SPEC] * 5,
            out_specs=[VMEM_SPEC] * 4,
            compiler_params=small,
            name="roles",
            cost_estimate=cost(0.6),
        )(*args)

    def obs_of(observed):
        return pl.pallas_call(
            obs_kernel,
            out_shape=jax.ShapeDtypeStruct((2, sensors, 2 * members), BF16),
            in_specs=[VMEM_SPEC],
            out_specs=VMEM_SPEC,
            compiler_params=small,
            name="observed",
            cost_estimate=cost(0.4),
        )(observed)

    def halves_of(far_state):
        return pl.pallas_call(
            halves_kernel,
            out_shape=jax.ShapeDtypeStruct((bins, 3 * members, cells), BF16),
            in_specs=[HBM_SPEC],
            out_specs=VMEM_SPEC,
            scratch_shapes=staging,
            compiler_params=small,
            name="halves",
            cost_estimate=cost(1.5),
        )(pltpu.with_memory_space_constraint(far_state, pltpu.HBM))

    made = {}

    def first_work():
        made["roles"] = roles_of(who, orders, inverse, places, weights, bin_response.T)
        made["near"] = spread_of(0, who, *made["roles"][1:3])

    def second_work():
        made["far"] = spread_of(half, who, *made["roles"][1:3])

    def third_work():
        made["parts"] = halves_of(state)
        made["obs"] = obs_of(observed.T)

    beside = [first_work, second_work, third_work]
    for i, group in enumerate(rounds):
        masks = [1 << bit for bit in group]
        if len(masks) == 2:
            masks.append(masks[0] | masks[1])
        if i == 0:
            piece, orders, places, weights = lax.optimization_barrier(
                (piece, orders, places, weights)
            )
        elif i == 1:
            piece, who = lax.optimization_barrier((piece, who))
        elif i == 2:
            piece, state, observed = lax.optimization_barrier((piece, state, observed))
        others = [exchange(piece, mask) for mask in masks]
        if i < len(beside):
            beside[i]()
        others, made = lax.optimization_barrier((others, made))
        piece = jnp.concatenate([piece] + others, axis=0)
    weight, _, _, resp = made["roles"]
    other = exchange(piece, 1)

    left = pltpu.VMEM((rows, 3 * half), BF16)
    hx = pl.pallas_call(
        functools.partial(partial_kernel, members, bins),
        out_shape=jax.ShapeDtypeStruct((members, width), F32),
        in_specs=[VMEM_SPEC] * 3,
        out_specs=VMEM_SPEC,
        scratch_shapes=[left],
        compiler_params=large,
        name="partial",
        cost_estimate=cost(1.2),
    )(piece, made["near"], resp)

    field, finals = pl.pallas_call(
        functools.partial(update_kernel, members, bins),
        out_shape=[
            jax.ShapeDtypeStruct((members, bins, cells), F32),
            jax.ShapeDtypeStruct((batches * share, members), F32),
        ],
        in_specs=[VMEM_SPEC] * 7,
        out_specs=[HBM_SPEC, HBM_SPEC],
        scratch_shapes=[
            left,
            pltpu.VMEM((2 * members, sensors), F32),
            pltpu.VMEM((bins, members, cells), F32),
            pltpu.VMEM((batches * share, members), F32),
            pltpu.SemaphoreType.DMA((bins + 1,)),
        ],
        compiler_params=large,
        name="update",
    )(hx, other, made["far"], resp, made["obs"], weight, made["parts"])
    return (field, finals.reshape(batches, share, members).transpose(0, 2, 1))


def solution(mesh):
    return jax.shard_map(
        shards,
        mesh=mesh,
        in_specs=(
            P(None, None, AXES),
            P(AXES),
            P(),
            P(),
            P(),
            P(),
            P(),
            P(),
        ),
        out_specs=(P(None, None, AXES), P(None, None, AXES)),
        check_vma=False,
    )
```

```python
import functools

import jax
import jax.numpy as jnp
from jax import lax
from jax.experimental import pallas as pl
from jax.experimental.pallas import tpu as pltpu
from jax.sharding import PartitionSpec as P

BLK = 128
P_SIZE = 1024
AXES = ("zrow", "zcol")
F32 = jnp.float32
BF16 = jnp.bfloat16
NT = (((1,), (1,)), ((), ()))
VMEM_SPEC = pl.BlockSpec(memory_space=pltpu.VMEM)
HBM_SPEC = pl.BlockSpec(memory_space=pltpu.HBM)
SMEM_SPEC = pl.BlockSpec(memory_space=pltpu.SMEM)
MIB = 1024 * 1024


def split(x):
    hi = x.astype(BF16)
    return hi, (x - hi.astype(F32)).astype(BF16)


def mm(a, b):
    ahi, alo = split(a)
    bhi, blo = split(b)
    return (
        jnp.dot(ahi, bhi, preferred_element_type=F32)
        + jnp.dot(ahi, blo, preferred_element_type=F32)
        + jnp.dot(alo, bhi, preferred_element_type=F32)
    )


def sublane_mean(x):
    return jnp.sum(x, axis=0, keepdims=True) * (1.0 / x.shape[0])


def lane_mean(x):
    return jnp.sum(x, axis=1, keepdims=True) * (1.0 / x.shape[1])


def means_kernel(x_ref, kernel_ref, out_ref, held_ref, sems, weight_ref, sem):
    members, bins, _ = x_ref.shape
    nb = out_ref.shape[0]
    kernel_copy = pltpu.make_async_copy(kernel_ref, weight_ref, sem)
    kernel_copy.start()
    copies = []
    for b in range(bins):
        copies.append(pltpu.make_async_copy(x_ref.at[:, b, :], held_ref.at[b], sems.at[b]))
        copies[-1].start()
    kernel_copy.wait()
    scale = weight_ref[...] * (1.0 / BLK)
    lane = lax.broadcasted_iota(jnp.int32, (2 * members, 128), 1)
    for b in range(0, bins, 2):
        copies[b].wait()
        copies[b + 1].wait()
        total = jnp.zeros((2 * members, 128), F32)
        for j in range(nb):
            cut = slice(j * BLK, (j + 1) * BLK)
            x = jnp.concatenate([held_ref[b, :, cut], held_ref[b + 1, :, cut]], axis=0)
            summed = jnp.sum(x * scale[:, cut], axis=1, keepdims=True)
            total = jnp.where(lane == j, summed, total)
        out_ref[:, b * members : (b + 2) * members] = total.T[0:nb, :]


def spread_kernel(bits, nb, first, me_ref, blocks_ref, weight_ref, out_ref):
    foot, sensors = blocks_ref.shape
    half = out_ref.shape[0] // 3
    step = 128
    for c in range(0, sensors, step):
        blk = blocks_ref[:, c : c + step]
        away = lax.shift_right_logical(blk, nb.bit_length() - 1) ^ me_ref[0]
        place = blk & (nb - 1)
        for i, bit in enumerate(bits):
            place += (lax.shift_right_logical(away, bit) & 1) * (nb << i)
        weight = weight_ref[:, c : c + step]
        for r in range(0, half, 128):
            row = lax.broadcasted_iota(jnp.int32, (128, step), 0) + (r + first)
            total = jnp.where(row == place[0:1, :], weight[0:1, :], 0.0)
            for f in range(1, foot):
                total += jnp.where(row == place[f : f + 1, :], weight[f : f + 1, :], 0.0)
            hi, low = split(total)
            out_ref[r : r + 128, c : c + step] = hi
            out_ref[half + r : half + r + 128, c : c + step] = low
            out_ref[2 * half + r : 2 * half + r + 128, c : c + step] = hi


def halves_kernel(x_ref, out_ref, held_ref, sems):
    members, bins, _ = x_ref.shape
    copies = []
    for b in range(bins):
        copies.append(pltpu.make_async_copy(x_ref.at[:, b, :], held_ref.at[b], sems.at[b]))
        copies[-1].start()
    for b in range(bins):
        copies[b].wait()
        hi, low = split(held_ref[b])
        out_ref[b, 0:members, :] = hi
        out_ref[b, members : 2 * members, :] = low
        out_ref[b, 2 * members : 3 * members, :] = hi


def roles_kernel(share, me_ref, orders_ref, var_ref, blocks_ref, foot_ref, resp_ref, weight_ref, *table_refs):
    batches = weight_ref.shape[0]
    groups = var_ref.shape[0]
    each = groups // batches
    per = each * 128
    sensors = blocks_ref.shape[1]
    start = me_ref[0] * share
    lane = lax.broadcasted_iota(jnp.int32, (8, 128), 1)
    own = jnp.full((8, 128), -1, jnp.int32)
    inverse = 1.0 / var_ref[...]
    high = lax.broadcasted_iota(jnp.int32, (groups, per), 0)
    low = lax.broadcasted_iota(jnp.int32, (128, per), 0)
    for t in range(batches):
        order = jnp.concatenate(
            [orders_ref[g : g + 1, :] for g in range(t * each, (t + 1) * each)], axis=1
        )
        mine = orders_ref[pl.ds(t * each + lax.shift_right_logical(start, 7), 1), :]
        mine = pltpu.roll(
            jnp.broadcast_to(mine, (8, 128)), (t * share - (start & 127)) & 127, axis=1
        )
        own = jnp.where((lane >= t * share) & (lane < (t + 1) * share), mine, own)
        of_high = jnp.where(high == lax.shift_right_logical(order, 7), 1.0, 0.0).astype(BF16)
        of_low = jnp.where(low == (order & 127), 1.0, 0.0).astype(BF16)
        held = lax.dot_general(of_high, of_low, NT, preferred_element_type=F32) * inverse
        for g in range(groups):
            weight_ref[t : t + 1, g * 128 : (g + 1) * 128] = held[g : g + 1, :]
    sensor = lax.broadcasted_iota(jnp.int32, (sensors, 128), 0)
    pick = jnp.where(sensor == own[0:1, :], 1.0, 0.0).astype(BF16)
    tables = jnp.concatenate(
        [blocks_ref[...].astype(F32), foot_ref[...], resp_ref[...]], axis=0
    )
    first = tables.astype(BF16)
    rest = tables - first.astype(F32)
    second = rest.astype(BF16)
    third = (rest - second.astype(F32)).astype(BF16)
    stacked = jnp.dot(
        jnp.concatenate([first, second, third], axis=0), pick, preferred_element_type=F32
    )
    n = tables.shape[0]
    chosen = stacked[0:n] + stacked[n : 2 * n] + stacked[2 * n : 3 * n]
    at = 0
    for ref, table in zip(table_refs, (blocks_ref, foot_ref, resp_ref)):
        rows = table.shape[0]
        ref[:, 0:sensors] = table[...]
        ref[:, sensors : sensors + 128] = chosen[at : at + rows].astype(ref.dtype)
        at += rows


def obs_kernel(obs_ref, out_ref):
    members = obs_ref.shape[0]
    step = 128
    for c in range(0, obs_ref.shape[1], step):
        turned = obs_ref[:, c : c + step].T
        hi, low = split(jnp.concatenate([jnp.zeros_like(turned), turned], axis=1))
        out_ref[0, c : c + step, :] = hi
        out_ref[1, c : c + step, :] = low


def turn(gathered_ref, left):
    half = gathered_ref.shape[0]
    for r in range(0, half, 128):
        hi, low = split(gathered_ref[r : r + 128, :].T)
        left[:, r : r + 128] = hi
        left[:, half + r : half + r + 128] = hi
        left[:, 2 * half + r : 2 * half + r + 128] = low


def observe(members, bins, left, spread_ref, resp_ref, cut):
    z = jnp.dot(left[...], spread_ref[:, cut], preferred_element_type=F32)
    hx = z[0:members, :] * resp_ref[0:1, cut]
    for b in range(1, bins):
        hx += z[b * members : (b + 1) * members, :] * resp_ref[b : b + 1, cut]
    return hx


def partial_kernel(members, bins, gathered_ref, spread_ref, resp_ref, hx_ref, left):
    turn(gathered_ref, left)
    width = resp_ref.shape[1]
    for c in range(0, width, 512):
        cut = slice(c, min(c + 512, width))
        hx_ref[:, cut] = observe(members, bins, left, spread_ref, resp_ref, cut)


def solve(aug):
    n, width = aug.shape
    p = 16
    blocks = n // p
    rows = [aug[p * i : p * i + p, :] for i in range(blocks)]
    sub = lax.broadcasted_iota(jnp.int32, (p, width), 0)

    def lanes(x, j):
        return jnp.broadcast_to(x[:, j : j + 1], (p, width))

    for k in range(blocks):
        piv = rows[k]
        own = [lanes(piv, p * k + q) for q in range(p)]
        for q in range(p):
            here = sub == q
            mult = own[q]
            inv = 1.0 / mult[q : q + 1, :]
            scaled = piv[q : q + 1, :] * inv
            piv = jnp.where(here, scaled, piv - mult * scaled)
            for r in range(q + 1, p):
                scaled = own[r][q : q + 1, :] * inv
                own[r] = jnp.where(here, scaled, own[r] - mult * scaled)
        for i in list(range(k + 1, blocks)) + list(range(k)):
            new = rows[i]
            for q in range(p):
                new = new - lanes(rows[i], p * k + q) * piv[q : q + 1, :]
            rows[i] = new
        rows[k] = piv
    return jnp.concatenate(rows, axis=0)


def update_kernel(
    members, bins, hx_ref, gathered_ref, spread_ref, resp_ref, obs_ref, weight_ref, x_ref,
    field_ref, finals_ref, left, anom, out, own, sems,
):
    sensors = weight_ref.shape[1]
    turn(gathered_ref, left)
    step = 512
    for c in range(0, sensors, step):
        cut = slice(c, c + step)
        hx = hx_ref[:, cut] + observe(members, bins, left, spread_ref, resp_ref, cut)
        center = sublane_mean(hx)
        anom[0:members, cut] = hx - center
        anom[members:, cut] = jnp.broadcast_to(center, (members, step))
    rhi, rlo = split(anom[...])
    whi, wlo = split(
        jnp.concatenate([anom[0:members, :] * weight_ref[t : t + 1, :] for t in range(2)], axis=0)
    )
    sums = (
        lax.dot_general(whi, rhi, NT, preferred_element_type=F32)
        + lax.dot_general(wlo, rhi, NT, preferred_element_type=F32)
        + lax.dot_general(whi, rlo, NT, preferred_element_type=F32)
    )
    pulls = (
        jnp.dot(whi, obs_ref[0], preferred_element_type=F32)
        + jnp.dot(wlo, obs_ref[0], preferred_element_type=F32)
        + jnp.dot(whi, obs_ref[1], preferred_element_type=F32)
    )
    lane = lax.broadcasted_iota(jnp.int32, (2 * members, 2 * members), 1)
    base = jnp.where(lane < members, sums, pulls - sums)
    lane = lane[0:members]
    right = lane >= members
    row = lax.broadcasted_iota(jnp.int32, lane.shape, 0)
    prior = jnp.where((lane == row) | (lane == row + members), members - 1.0, 0.0)
    even = jnp.where(right, 1.0 / members, 0.0)

    def mixer_t(solved):
        held = jnp.where(right, solved, 0.0)
        return held - sublane_mean(held) + even

    first_t = mixer_t(solve(base[0:members] + prior))
    tilt = jnp.sum(first_t, axis=1, keepdims=True) * (1.0 / members)
    first = first_t.T[members:, :]
    first_c = first - sublane_mean(first)
    moved = mm(first_c, base[members:])
    swapped = pltpu.roll(first_t, members, axis=1) - tilt
    crossed = mm(moved[:, 0:members], jnp.where(right, tilt, swapped))
    second_t = mixer_t(
        solve(prior + jnp.where(right, moved - crossed, crossed))
    )
    total = mm(second_t.T[members:, :], jnp.concatenate([first, first], axis=1))
    thi, tlo = split(total)
    lhs = jnp.concatenate([thi, tlo[:, 0:members]], axis=1)
    copies = []
    for group in (range(0, bins // 4), range(bins // 4, bins)):
        for b in group:
            out[b] = jnp.dot(lhs, x_ref[b], preferred_element_type=F32)
        for b in group:
            copies.append(pltpu.make_async_copy(out.at[b], field_ref.at[:, b, :], sems.at[b]))
            copies[-1].start()
    cut = slice(sensors, sensors + 128)
    picked = hx_ref[:, cut] + observe(members, bins, left, spread_ref, resp_ref, cut)
    own[...] = mm(total[:, 0:members], picked).T[0 : own.shape[0], :]
    copies.append(pltpu.make_async_copy(own, finals_ref, sems.at[bins]))
    copies[-1].start()
    for copy in copies:
        copy.wait()


def shards(state, kernel, blocks, foot_weight, bin_response, observed, obs_var, batch_order):
    members, bins, cells = state.shape
    nb = cells // BLK
    sensors = obs_var.shape[0]
    batches = sensors // P_SIZE
    nz, nc = lax.axis_size("zrow"), lax.axis_size("zcol")
    devices = nz * nc
    me = lax.axis_index(AXES)
    share = P_SIZE // devices
    zbits = [(nc << i).bit_length() - 1 for i in range(nz.bit_length() - 1)]
    cbits = [i for i in reversed(range(nc.bit_length() - 1))]
    rounds = [[bit] for bit in reversed(zbits)]
    plane = [bit for bit in cbits if bit > 0]
    while plane:
        rounds.append(sorted(plane[-2:]))
        plane = plane[:-2]
    bits = [bit for group in rounds for bit in group] + [0]
    rows = members * bins
    half = nb * devices // 2
    wide = 6 * half * sensors
    width = sensors + 128
    small = pltpu.CompilerParams(vmem_limit_bytes=8 * MIB + wide)
    large = pltpu.CompilerParams(vmem_limit_bytes=12 * MIB + 2 * wide)

    def cost(us):
        return pl.CostEstimate(flops=0, bytes_accessed=int(us * 3000000), transcendentals=0)

    def spread_of(first, who, places, weights):
        return pl.pallas_call(
            functools.partial(spread_kernel, bits, nb, first),
            out_shape=jax.ShapeDtypeStruct((3 * half, width), BF16),
            in_specs=[SMEM_SPEC, VMEM_SPEC, VMEM_SPEC],
            out_specs=VMEM_SPEC,
            compiler_params=small,
            name="spread",
            cost_estimate=cost(1.0),
        )(who, places, weights)

    def exchange(value, mask):
        return lax.ppermute(value, AXES, [(i, i ^ mask) for i in range(devices)])

    far_state = pltpu.with_memory_space_constraint(state, pltpu.HBM)
    staging = [pltpu.VMEM((bins, members, cells), F32), pltpu.SemaphoreType.DMA((bins,))]
    piece = pl.pallas_call(
        means_kernel,
        out_shape=jax.ShapeDtypeStruct((nb, rows), F32),
        in_specs=[HBM_SPEC, HBM_SPEC],
        out_specs=VMEM_SPEC,
        scratch_shapes=staging + [pltpu.VMEM((1, cells), F32), pltpu.SemaphoreType.DMA],
        compiler_params=small,
        name="means",
    )(far_state, pltpu.with_memory_space_constraint(kernel.reshape(1, cells), pltpu.HBM))

    who, places, weights = me.reshape(1), blocks.T, foot_weight.T
    orders = batch_order.reshape(sensors // 128, 128)
    inverse = obs_var.reshape(sensors // 128, 128)

    def roles_of(*args):
        return pl.pallas_call(
            functools.partial(roles_kernel, share),
            out_shape=[
                jax.ShapeDtypeStruct((batches, sensors), F32),
                jax.ShapeDtypeStruct((blocks.shape[1], width), jnp.int32),
                jax.ShapeDtypeStruct((blocks.shape[1], width), F32),
                jax.ShapeDtypeStruct((bins, width), F32),
            ],
            in_specs=[SMEM_SPEC] + [VMEM_SPEC] * 5,
            out_specs=[VMEM_SPEC] * 4,
            compiler_params=small,
            name="roles",
            cost_estimate=cost(0.6),
        )(*args)

    def obs_of(observed):
        return pl.pallas_call(
            obs_kernel,
            out_shape=jax.ShapeDtypeStruct((2, sensors, 2 * members), BF16),
            in_specs=[VMEM_SPEC],
            out_specs=VMEM_SPEC,
            compiler_params=small,
            name="observed",
            cost_estimate=cost(0.4),
        )(observed)

    def halves_of(far_state):
        return pl.pallas_call(
            halves_kernel,
            out_shape=jax.ShapeDtypeStruct((bins, 3 * members, cells), BF16),
            in_specs=[HBM_SPEC],
            out_specs=VMEM_SPEC,
            scratch_shapes=staging,
            compiler_params=small,
            name="halves",
            cost_estimate=cost(1.5),
        )(pltpu.with_memory_space_constraint(far_state, pltpu.HBM))

    made = {}

    def first_work():
        made["roles"] = roles_of(who, orders, inverse, places, weights, bin_response.T)
        made["near"] = spread_of(0, who, *made["roles"][1:3])

    def second_work():
        made["far"] = spread_of(half, who, *made["roles"][1:3])

    def third_work():
        made["parts"] = halves_of(state)
        made["obs"] = obs_of(observed.T)

    beside = [first_work, second_work, third_work]
    for i, group in enumerate(rounds):
        masks = [1 << bit for bit in group]
        if len(masks) == 2:
            masks.append(masks[0] | masks[1])
        if i == 0:
            piece, orders, places, weights = lax.optimization_barrier(
                (piece, orders, places, weights)
            )
        elif i == 1:
            piece, who = lax.optimization_barrier((piece, who))
        elif i == 2:
            piece, state, observed = lax.optimization_barrier((piece, state, observed))
        others = [exchange(piece, mask) for mask in masks]
        if i < len(beside):
            beside[i]()
        others, made = lax.optimization_barrier((others, made))
        piece = jnp.concatenate([piece] + others, axis=0)
    weight, _, _, resp = made["roles"]
    other = exchange(piece, 1)

    left = pltpu.VMEM((rows, 3 * half), BF16)
    hx = pl.pallas_call(
        functools.partial(partial_kernel, members, bins),
        out_shape=jax.ShapeDtypeStruct((members, width), F32),
        in_specs=[VMEM_SPEC] * 3,
        out_specs=VMEM_SPEC,
        scratch_shapes=[left],
        compiler_params=large,
        name="partial",
        cost_estimate=cost(1.2),
    )(piece, made["near"], resp)

    field, finals = pl.pallas_call(
        functools.partial(update_kernel, members, bins),
        out_shape=[
            jax.ShapeDtypeStruct((members, bins, cells), F32),
            jax.ShapeDtypeStruct((batches * share, members), F32),
        ],
        in_specs=[VMEM_SPEC] * 7,
        out_specs=[HBM_SPEC, HBM_SPEC],
        scratch_shapes=[
            left,
            pltpu.VMEM((2 * members, sensors), F32),
            pltpu.VMEM((bins, members, cells), F32),
            pltpu.VMEM((batches * share, members), F32),
            pltpu.SemaphoreType.DMA((bins + 1,)),
        ],
        compiler_params=large,
        name="update",
    )(hx, other, made["far"], resp, made["obs"], weight, made["parts"])
    return (field, finals.reshape(batches, share, members).transpose(0, 2, 1))


def solution(mesh):
    return jax.shard_map(
        shards,
        mesh=mesh,
        in_specs=(
            P(None, None, AXES),
            P(AXES),
            P(),
            P(),
            P(),
            P(),
            P(),
            P(),
        ),
        out_specs=(P(None, None, AXES), P(None, None, AXES)),
        check_vma=False,
    )
```
